32 devices in a mesh: grp: 2 (over y), seq: 4 (over x, core), head: 4 (over z).
Axes of the slice: x: 2, y: 2, z: 4, core: 2. Of those that a mesh axis runs over, the one named last changes fastest.
Arguments:
- activations: bfloat16 [16384, 2048], P(('grp', 'seq')), parts along dimension 0, may hold values from -6 to 6
- w_query: bfloat16 [2048, 2048], P(None, 'head'), may hold values from -0.125 to 0.125
- w_key: bfloat16 [2048, 2048], P(None, 'head'), may hold values from -0.125 to 0.125
- w_value: bfloat16 [2048, 2048], P(None, 'head'), may hold values from -0.125 to 0.125
- w_out: bfloat16 [2048, 2048], P('head', 'seq'), may hold values from -0.125 to 0.125
- log_decay: float32 [16, 16384], P('head', ('grp', 'seq')), parts along dimension 1, may hold values from -3 to 0, as said below
Outputs:
- mixed: bfloat16 [16384, 2048], P(('grp', 'seq', 'head')), parts along dimension 0
The draws below stay inside these ranges and needn't reach their ends.
There are 2 independent parts, one for each index of `grp`. The reference program is written for one: setup_inputs(seed, part) draws one part's arguments, and reference() takes and returns one part's arrays. A program takes and returns all parts, laid end to end along the dimension named above; an argument that names none is the same for every part. Nothing has to cross between parts.
Inputs may be any that keep to these rules, and one draw needn't show every extreme that they name: `log_decay`: never positive.
All inputs are finite; a program needn't handle non-finite values.
Results may differ from the reference program's by a relative error of at most 0.0067.
Values may be sent and summed in bfloat16 or wider, within the bound.
No kernel may reach another device: no remote copies, remote signals or barrier semaphores. Data moves between devices by JAX's collectives and lax.ppermute only.
A program may use at most 128 MiB of HBM per device.

```python
import jax
import jax.numpy as jnp
from jax import lax

D = 2048
HEAD_COUNT = 16
DH = 128
BLOCK = 256
TOK_DEV = 2048
TOKEN_COUNT = 8192


def draw_log_decay(key, part):
    random_subkeys = jax.random.split(jax.random.fold_in(key, 17), 7)
    fast_share = 0.5
    is_fast = jax.random.uniform(random_subkeys[0], (HEAD_COUNT, 1)) < fast_share
    fast_rate = 0.025 * jnp.exp(jax.random.uniform(random_subkeys[1], (HEAD_COUNT, 1), minval=-0.3, maxval=0.3))
    slow_rate = 0.7 / TOKEN_COUNT * jax.random.uniform(random_subkeys[2], (HEAD_COUNT, 1), minval=0.5, maxval=1.5)
    baseline_rate = jnp.where(is_fast, fast_rate, slow_rate)
    groups_count = TOKEN_COUNT // TOK_DEV
    machine_multiplier = jnp.exp(jax.random.uniform(random_subkeys[3], (HEAD_COUNT, groups_count, 1), minval=-0.35, maxval=0.35))
    machine_multiplier = jnp.broadcast_to(machine_multiplier, (HEAD_COUNT, groups_count, TOK_DEV)).reshape(HEAD_COUNT, TOKEN_COUNT)
    random_noise = jax.random.uniform(random_subkeys[4], (HEAD_COUNT, TOKEN_COUNT), minval=0.5, maxval=1.5)
    spike_position = jax.random.randint(random_subkeys[5], (HEAD_COUNT, 3), 0, TOKEN_COUNT)
    spike_decrease = jnp.log(jax.random.uniform(random_subkeys[6], (HEAD_COUNT, 3), minval=0.5, maxval=0.8))
    token_positions = jnp.arange(TOKEN_COUNT)
    spike_events = jnp.sum(jnp.where(token_positions[None, None, :] == spike_position[:, :, None], spike_decrease[:, :, None], 0.0), axis=1)
    return (-(baseline_rate * machine_multiplier * random_noise) + spike_events).astype(jnp.float32)


def shard_levels(own_key, dims, shards, least, high):
    level, own = 1.0, jax.random.fold_in(own_key, 6)
    for axis_at, blocks in shards:
        heights = jnp.exp(jax.random.uniform(jax.random.fold_in(own, axis_at), (blocks,), jnp.float32, least / len(shards), high / len(shards)))
        level = level * jnp.repeat(heights, dims[axis_at] // blocks).reshape([-1 if axis == axis_at else 1 for axis in range(len(dims))])
    return level


def centred(key, extent, spread, reach, pieces=(), dtype=jnp.bfloat16):
    values = jax.random.normal(key, extent, jnp.float32) * spread
    if len(pieces) > 0:
        values = shard_levels(key, extent, pieces, -0.22, 0.18) * values
    return jnp.clip(values, min=-reach, max=reach).astype(dtype)


def setup_inputs(seed: int = 0, part: int = 0) -> dict:
    keys = jax.random.split(jax.random.key(seed), 7)
    part_keys = jax.random.split(jax.random.fold_in(keys[6], part), 7)
    return {
        "activations": centred(part_keys[0], (TOKEN_COUNT, D), 1.0, 6.0, ((0, 4),)),
        "w_query": centred(keys[1], (D, D), D ** -0.5, 0.125, ((1, 4),)),
        "w_key": centred(keys[2], (D, D), D ** -0.5, 0.125, ((1, 4),)),
        "w_value": centred(keys[3], (D, D), D ** -0.5, 0.125, ((1, 4),)),
        "w_out": centred(keys[4], (D, D), D ** -0.5, 0.125, ((0, 4), (1, 4))),
        "log_decay": draw_log_decay(jax.random.fold_in(jax.random.fold_in(keys[6], part), 71), part),
    }


HIGHEST = lax.Precision.HIGHEST

def reference(activations, w_query, w_key, w_value, w_out, log_decay):
    query = jnp.dot(activations, w_query, preferred_element_type=jnp.float32).astype(jnp.bfloat16)
    key_proj = jnp.dot(activations, w_key, preferred_element_type=jnp.float32).astype(jnp.bfloat16)
    value_proj = jnp.dot(activations, w_value, preferred_element_type=jnp.float32).astype(jnp.bfloat16)
    blocks = TOKEN_COUNT // BLOCK

    def to_blocks(array):
        return array.reshape(blocks, BLOCK, HEAD_COUNT, DH)
    decays = log_decay.reshape(HEAD_COUNT, blocks, BLOCK).transpose(1, 0, 2)
    causal = jnp.arange(BLOCK)[:, None] >= jnp.arange(BLOCK)[None, :]

    def advance(carried, inputs_now):
        query_block, key_block, value_block, decay_block = inputs_now
        query_wide = query_block.astype(jnp.float32)
        key_wide = key_block.astype(jnp.float32)
        value_wide = value_block.astype(jnp.float32)
        within = jnp.cumsum(decay_block, axis=1)
        spread_log = within[:, :, None] - within[:, None, :]
        decay_mask = jnp.where(causal, jnp.exp(jnp.minimum(spread_log, 0.0)), 0.0)
        scores = jnp.einsum('thd,shd->hts', query_block, key_block, preferred_element_type=jnp.float32)
        within_block = jnp.einsum('hts,shd->thd', scores * decay_mask, value_wide, precision=HIGHEST)
        across_block = jnp.einsum('ht,thd,hde->the', jnp.exp(within), query_wide, carried, precision=HIGHEST)
        block_total = within[:, -1]
        carry_weight = jnp.exp(block_total[:, None] - within)
        update_sum = jnp.einsum('hs,shd,she->hde', carry_weight, key_wide, value_wide, precision=HIGHEST)
        updated = jnp.exp(block_total)[:, None, None] * carried + update_sum
        return (updated, within_block + across_block)
    initial = jnp.zeros((HEAD_COUNT, DH, DH), jnp.float32)
    _, outputs = lax.scan(advance, initial, (to_blocks(query), to_blocks(key_proj), to_blocks(value_proj), decays))
    attended = outputs.reshape(TOKEN_COUNT, HEAD_COUNT, DH)
    normed = attended * lax.rsqrt(lax.optimization_barrier(jnp.mean(attended * attended, axis=-1, keepdims=True)) + 1e-05)
    normed = normed.astype(jnp.bfloat16).reshape(TOKEN_COUNT, D)
    return jnp.dot(normed, w_out, preferred_element_type=jnp.float32).astype(jnp.bfloat16)
```

```python
import functools

import jax
import jax.numpy as jnp
from jax import lax
from jax.experimental import pallas as pl
from jax.experimental.pallas import tpu as pltpu
from jax.sharding import PartitionSpec as P

DH = 128
BLOCK = 256
STEP = 512
EXTRA = 16
CHUNKS = ((0, 2), (2, 4))
F32 = jnp.float32
BF16 = jnp.bfloat16
HIGHEST = lax.Precision.HIGHEST
MIB = 1 << 20


def dot(a, b, dims=((1,), (0,)), precision=None):
    return lax.dot_general(a, b, (dims, ((), ())), precision=precision, preferred_element_type=F32)


def relative_half(part, width):
    start = lax.rem(part + lax.axis_index("grp"), 2) * width
    return pl.ds(pl.multiple_of(start, width), width)


def kv_kernel(act, wk, wv, decay, k_out, v_out, before, payload, wcol, wrow, state, factor):
    step = pl.program_id(0)
    heads, tokens = decay.shape
    blocks = tokens // BLOCK
    half = heads // 2

    @pl.when(step == 0)
    def _():
        logs = decay[...]
        swapped = jnp.concatenate([logs[half:], logs[:half]], axis=0)
        logs = jnp.where(lax.axis_index("grp") == 0, logs, swapped)
        logs = jnp.concatenate([logs, jnp.zeros((8 - heads, tokens), F32)], axis=0)
        stacked = jnp.concatenate(
            [logs[:, n * BLOCK : (n + 1) * BLOCK] for n in range(blocks)], axis=0
        )
        upper = (
            lax.broadcasted_iota(jnp.int32, (BLOCK, BLOCK), 0)
            <= lax.broadcasted_iota(jnp.int32, (BLOCK, BLOCK), 1)
        ).astype(F32)
        within = dot(stacked, upper, precision=HIGHEST)
        total = jnp.zeros((8, 1), F32)
        for n in range(blocks):
            rows = within[n * 8 : (n + 1) * 8]
            wrow[n] = rows
            wcol[n] = rows.T
            total = total + rows[:, BLOCK - 1 :]
        factor[...] = jnp.broadcast_to(jnp.exp(total), (8, DH))
        state[...] = jnp.zeros_like(state)

    rows = act[...]
    k_halves, v_halves = [], []
    for part in range(2):
        columns = relative_half(part, half * DH)
        k_halves.append(dot(rows, wk[:, columns]).astype(BF16))
        v_halves.append(dot(rows, wv[:, columns]).astype(BF16))
        k_out[:, part * half * DH : (part + 1) * half * DH] = k_halves[part]
        v_out[:, part * half * DH : (part + 1) * half * DH] = v_halves[part]
    for b in range(STEP // BLOCK):
        cols = wcol[step * (STEP // BLOCK) + b]
        last = cols[BLOCK - 1 :]
        carry = jnp.exp(last - cols)
        shrink = jnp.exp(last)
        for h in range(heads):
            part, lane = h // half, (h % half) * DH
            k_b = k_halves[part][b * BLOCK : (b + 1) * BLOCK, lane : lane + DH]
            v_b = v_halves[part][b * BLOCK : (b + 1) * BLOCK, lane : lane + DH]
            k_b = (k_b.astype(F32) * carry[:, h : h + 1]).astype(BF16)
            update = dot(k_b, v_b, ((0,), (0,)))
            old = state[h]
            before[b, h] = old
            state[h] = shrink[:, h : h + 1] * old + update

    @pl.when(step == pl.num_programs(0) - 1)
    def _():
        for h in range(heads):
            payload[h, :DH] = state[h].astype(BF16)
            whole = jnp.broadcast_to(factor[h : h + 1], (EXTRA, DH))
            high = whole.astype(BF16).astype(F32)
            first = lax.broadcasted_iota(jnp.int32, (EXTRA, DH), 0) < EXTRA // 2
            payload[h, DH:] = jnp.where(first, high, whole - high).astype(BF16)


def project_kernel(act, w, out):
    half = out.shape[1] // 2
    rows = act[...]
    for part in range(2):
        columns = relative_half(part, half)
        out[:, part * half : (part + 1) * half] = dot(rows, w[:, columns]).astype(BF16)


def attend_kernel(first, count, received, q, k, v, before, wcol, wrow, *rest):
    arrivals, (out, prefix) = rest[:received], rest[received:]
    heads = range(first, first + count)

    @pl.when(pl.program_id(0) == 0)
    def _():
        for at, h in enumerate(heads):
            total = jnp.zeros((DH, DH), F32)
            reach = jnp.ones((1, DH), F32)
            for piece in arrivals:
                total = total + reach * piece[h, :DH].astype(F32)
                extra = piece[h, DH:].astype(F32)
                reach = reach * (extra[:1] + extra[EXTRA // 2 : EXTRA // 2 + 1])
            prefix[at] = total

    causal = lax.broadcasted_iota(jnp.int32, (BLOCK, BLOCK), 0) >= lax.broadcasted_iota(
        jnp.int32, (BLOCK, BLOCK), 1
    )
    for b in range(STEP // BLOCK):
        tokens = slice(b * BLOCK, (b + 1) * BLOCK)
        cols = wcol[b]
        grown = jnp.exp(cols)
        for at, h in enumerate(heads):
            lanes = slice(h * DH, (h + 1) * DH)
            q_b, k_b, v_b = q[tokens, lanes], k[tokens, lanes], v[tokens, lanes]
            spread = cols[:, h : h + 1] - wrow[b, h : h + 1]
            mask = jnp.exp(jnp.where(causal, jnp.minimum(spread, 0.0), -1e30))
            scores = (dot(q_b, k_b, ((1,), (1,))) * mask).astype(BF16)
            reached = (q_b.astype(F32) * grown[:, h : h + 1]).astype(BF16)
            carried = prefix[at]
            incoming = (before[b, h] + carried).astype(BF16)
            attended = dot(scores, v_b) + dot(reached, incoming)
            prefix[at] = carried * grown[BLOCK - 1 :, h : h + 1]
            mean = jnp.mean(attended * attended, axis=1, keepdims=True)
            out[tokens, at * DH : (at + 1) * DH] = (attended * lax.rsqrt(mean + 1e-5)).astype(BF16)


def out_kernel(plan, order, lead, features, *rest):
    if lead:
        earlier, rest = rest[0], rest[1:]
    weights, out = rest[:-1], rest[-1]
    mine, place = lax.axis_index("head"), lax.axis_index("seq")
    sources = features.shape[0]
    for offset, pieces in plan:
        total = None
        for at, first, count, lane, row, size, stride in pieces:
            for r in range(first, first + count):
                left = features[lax.bitwise_xor(mine, order[r]), :, lane : lane + size]
                start = (r - first) * stride + row
                term = dot(left, weights[at][start : start + size])
                total = term if total is None else total + term
        width = total.shape[1]
        columns = pl.ds(pl.multiple_of(lax.bitwise_xor(place, offset) * width, width), width)
        if lead:
            total = total + earlier[:, columns]
        out[:, columns] = total.astype(out.dtype)


def params(limit):
    return pltpu.CompilerParams(vmem_limit_bytes=limit, dimension_semantics=("arbitrary",))


def whole_block(shape):
    return pl.BlockSpec(shape, lambda i: (0,) * len(shape))


def keys_values(activations, w_key, w_value, log_decay):
    tokens, width = activations.shape
    heads = log_decay.shape[0]
    columns, blocks, inner = heads * DH, tokens // BLOCK, STEP // BLOCK
    row_block = pl.BlockSpec((STEP, columns), lambda i: (i, 0))
    return pl.pallas_call(
        kv_kernel,
        grid=(tokens // STEP,),
        in_specs=[
            pl.BlockSpec((STEP, width), lambda i: (i, 0)),
            whole_block((width, columns)),
            whole_block((width, columns)),
            whole_block((heads, tokens)),
        ],
        out_specs=[
            row_block,
            row_block,
            pl.BlockSpec((inner, heads, DH, DH), lambda i: (i, 0, 0, 0)),
            whole_block((heads, DH + EXTRA, DH)),
            whole_block((blocks, BLOCK, 8)),
            whole_block((blocks, 8, BLOCK)),
        ],
        out_shape=[
            jax.ShapeDtypeStruct((tokens, columns), BF16),
            jax.ShapeDtypeStruct((tokens, columns), BF16),
            jax.ShapeDtypeStruct((blocks, heads, DH, DH), F32),
            jax.ShapeDtypeStruct((heads, DH + EXTRA, DH), BF16),
            jax.ShapeDtypeStruct((blocks, BLOCK, 8), F32),
            jax.ShapeDtypeStruct((blocks, 8, BLOCK), F32),
        ],
        scratch_shapes=[pltpu.VMEM((heads, DH, DH), F32), pltpu.VMEM((8, DH), F32)],
        compiler_params=params(32 * MIB),
        name="keys_values",
    )(activations, w_key, w_value, log_decay)


def queries(activations, w_query):
    tokens, width = activations.shape
    columns = w_query.shape[1]
    return pl.pallas_call(
        project_kernel,
        grid=(tokens // STEP,),
        in_specs=[pl.BlockSpec((STEP, width), lambda i: (i, 0)), whole_block((width, columns))],
        out_specs=pl.BlockSpec((STEP, columns), lambda i: (i, 0)),
        out_shape=jax.ShapeDtypeStruct((tokens, columns), BF16),
        compiler_params=params(24 * MIB),
        name="queries",
    )(activations, w_query)


def attend(first, count, query, key, value, before, wcol, wrow, arrivals):
    tokens, columns = query.shape
    heads, inner = columns // DH, STEP // BLOCK
    row_block = pl.BlockSpec((STEP, columns), lambda i: (i, 0))
    return pl.pallas_call(
        functools.partial(attend_kernel, first, count, len(arrivals)),
        grid=(tokens // STEP,),
        in_specs=[
            row_block,
            row_block,
            row_block,
            pl.BlockSpec((inner, heads, DH, DH), lambda i: (i, 0, 0, 0)),
            pl.BlockSpec((inner, BLOCK, 8), lambda i: (i, 0, 0)),
            pl.BlockSpec((inner, 8, BLOCK), lambda i: (i, 0, 0)),
        ]
        + [whole_block(piece.shape) for piece in arrivals],
        out_specs=pl.BlockSpec((STEP, count * DH), lambda i: (i, 0)),
        out_shape=jax.ShapeDtypeStruct((tokens, count * DH), BF16),
        scratch_shapes=[pltpu.VMEM((count, DH, DH), F32)],
        compiler_params=params(24 * MIB),
        name="attend",
    )(query, key, value, before, wcol, wrow, *arrivals)


def swap(value, axis, bit):
    count = lax.axis_size(axis)
    return lax.ppermute(value, axis, [(i, i ^ bit) for i in range(count)])


def bits_of(count):
    return [1 << b for b in reversed(range(count.bit_length() - 1))]


def gather_rows(w_out):
    half = w_out.shape[0] // 2
    piece = lax.dynamic_slice_in_dim(w_out, lax.axis_index("grp") * half, half, axis=0)
    order = [0]
    for bit in bits_of(lax.axis_size("head")):
        piece = jnp.concatenate([piece, swap(piece, "head", bit)], axis=0)
        order = order + [r ^ bit for r in order]
    return piece, order


def gather_columns(piece):
    middle = piece.shape[0] // 2
    across, beside = swap(piece, "seq", 2), swap(piece, "grp", 1)
    corner = [swap(beside[:middle], "seq", 2), swap(across[middle:], "grp", 1)]
    found = {(0, 0): [piece], (0, 2): [across], (1, 0): [beside], (1, 2): corner}
    for bit in bits_of(lax.axis_size("seq"))[:-2]:
        found.update(
            {
                (g, s ^ bit): [swap(part, "seq", bit) for part in parts]
                for (g, s), parts in list(found.items())
            }
        )
    found.update(
        {(g, s ^ 1): [swap(part, "seq", 1) for part in parts] for (g, s), parts in found.items()}
    )
    return found


def project_out(features, found, order, first, count, heads, earlier, dtype):
    sources, rows, _ = features.shape
    half = heads // 2
    operands, plan = [], []
    for offset in sorted({s for _, s in found}):
        pieces = []
        for g in range(2):
            low, high = max(first, g * half), min(first + count, (g + 1) * half)
            if low >= high:
                continue
            done = 0
            for part in found[(g, offset)]:
                held = part.shape[0] // (half * DH)
                pieces.append((len(operands), done, held, (low - first) * DH, (low - g * half) * DH,
                               (high - low) * DH, half * DH))
                operands.append(part)
                done += held
        plan.append((offset, tuple(pieces)))
    width = sum(1 for _ in plan) * operands[0].shape[1]
    lead = [] if earlier is None else [earlier]
    return pl.pallas_call(
        functools.partial(out_kernel, tuple(plan), order, bool(lead)),
        out_shape=jax.ShapeDtypeStruct((rows, width), dtype),
        compiler_params=pltpu.CompilerParams(vmem_limit_bytes=40 * MIB),
        name="project_out",
    )(features, *lead, *operands)


def on_device(activations, w_query, w_key, w_value, w_out, log_decay):
    heads, tokens = log_decay.shape
    places, sources = lax.axis_size("seq"), lax.axis_size("head")
    rows, order = gather_rows(w_out)
    key, value, before, payload, wcol, wrow = keys_values(activations, w_key, w_value, log_decay)
    arrivals = [
        lax.ppermute(payload, "seq", [(i, i + r) for i in range(places - r)])
        for r in range(1, places)
    ]
    query = queries(activations, w_query)
    found = gather_columns(rows)
    chunks = CHUNKS if heads == 4 else ((0, heads),)
    mixed = None
    for first, last in chunks:
        normed = attend(first, last - first, query, key, value, before, wcol, wrow, arrivals)
        features = lax.all_to_all(
            normed.reshape(sources, tokens // sources, (last - first) * DH), "head", 0, 0
        )
        dtype = BF16 if last == heads else F32
        mixed = project_out(features, found, order, first, last - first, heads, mixed, dtype)
    return mixed


def solution(mesh):
    return jax.shard_map(
        on_device,
        mesh=mesh,
        in_specs=(
            P(("grp", "seq"), None),
            P(None, "head"),
            P(None, "head"),
            P(None, "head"),
            P("head", "seq"),
            P("head", ("grp", "seq")),
        ),
        out_specs=P(("grp", "seq", "head"), None),
        check_vma=False,
    )
```

```python
import functools

import jax
import jax.numpy as jnp
from jax import lax
from jax.experimental import pallas as pl
from jax.experimental.pallas import tpu as pltpu
from jax.sharding import PartitionSpec as P

DH = 128
BLOCK = 256
STEP = 512
EXTRA = 16
CHUNKS = ((0, 2), (2, 4))
F32 = jnp.float32
BF16 = jnp.bfloat16
HIGHEST = lax.Precision.HIGHEST
MIB = 1 << 20


def dot(a, b, dims=((1,), (0,)), precision=None):
    return lax.dot_general(a, b, (dims, ((), ())), precision=precision, preferred_element_type=F32)


def relative_half(part, width):
    start = lax.rem(part + lax.axis_index("grp"), 2) * width
    return pl.ds(pl.multiple_of(start, width), width)


def kv_kernel(act, wk, wv, decay, k_out, v_out, before, payload, wcol, wrow, state, factor):
    step = pl.program_id(0)
    heads, tokens = decay.shape
    blocks = tokens // BLOCK
    half = heads // 2

    @pl.when(step == 0)
    def _():
        logs = decay[...]
        swapped = jnp.concatenate([logs[half:], logs[:half]], axis=0)
        logs = jnp.where(lax.axis_index("grp") == 0, logs, swapped)
        logs = jnp.concatenate([logs, jnp.zeros((8 - heads, tokens), F32)], axis=0)
        stacked = jnp.concatenate(
            [logs[:, n * BLOCK : (n + 1) * BLOCK] for n in range(blocks)], axis=0
        )
        upper = (
            lax.broadcasted_iota(jnp.int32, (BLOCK, BLOCK), 0)
            <= lax.broadcasted_iota(jnp.int32, (BLOCK, BLOCK), 1)
        ).astype(F32)
        within = dot(stacked, upper, precision=HIGHEST)
        total = jnp.zeros((8, 1), F32)
        for n in range(blocks):
            rows = within[n * 8 : (n + 1) * 8]
            wrow[n] = rows
            wcol[n] = rows.T
            total = total + rows[:, BLOCK - 1 :]
        factor[...] = jnp.broadcast_to(jnp.exp(total), (8, DH))
        state[...] = jnp.zeros_like(state)

    rows = act[...]
    k_halves, v_halves = [], []
    for part in range(2):
        columns = relative_half(part, half * DH)
        k_halves.append(dot(rows, wk[:, columns]).astype(BF16))
        v_halves.append(dot(rows, wv[:, columns]).astype(BF16))
        k_out[:, part * half * DH : (part + 1) * half * DH] = k_halves[part]
        v_out[:, part * half * DH : (part + 1) * half * DH] = v_halves[part]
    for b in range(STEP // BLOCK):
        cols = wcol[step * (STEP // BLOCK) + b]
        last = cols[BLOCK - 1 :]
        carry = jnp.exp(last - cols)
        shrink = jnp.exp(last)
        for h in range(heads):
            part, lane = h // half, (h % half) * DH
            k_b = k_halves[part][b * BLOCK : (b + 1) * BLOCK, lane : lane + DH]
            v_b = v_halves[part][b * BLOCK : (b + 1) * BLOCK, lane : lane + DH]
            k_b = (k_b.astype(F32) * carry[:, h : h + 1]).astype(BF16)
            update = dot(k_b, v_b, ((0,), (0,)))
            old = state[h]
            before[b, h] = old
            state[h] = shrink[:, h : h + 1] * old + update

    @pl.when(step == pl.num_programs(0) - 1)
    def _():
        for h in range(heads):
            payload[h, :DH] = state[h].astype(BF16)
            whole = jnp.broadcast_to(factor[h : h + 1], (EXTRA, DH))
            high = whole.astype(BF16).astype(F32)
            first = lax.broadcasted_iota(jnp.int32, (EXTRA, DH), 0) < EXTRA // 2
            payload[h, DH:] = jnp.where(first, high, whole - high).astype(BF16)


def project_kernel(act, w, out):
    half = out.shape[1] // 2
    rows = act[...]
    for part in range(2):
        columns = relative_half(part, half)
        out[:, part * half : (part + 1) * half] = dot(rows, w[:, columns]).astype(BF16)


def attend_kernel(first, count, lane, received, q, k, v, before, wcol, wrow, *rest):
    arrivals, (out, prefix) = rest[:received], rest[received:]
    heads = range(first, first + count)

    @pl.when(pl.program_id(0) == 0)
    def _():
        for at, h in enumerate(heads):
            total = jnp.zeros((DH, DH), F32)
            reach = jnp.ones((1, DH), F32)
            for piece in arrivals:
                total = total + reach * piece[h, :DH].astype(F32)
                extra = piece[h, DH:].astype(F32)
                reach = reach * (extra[:1] + extra[EXTRA // 2 : EXTRA // 2 + 1])
            prefix[at] = total

    causal = lax.broadcasted_iota(jnp.int32, (BLOCK, BLOCK), 0) >= lax.broadcasted_iota(
        jnp.int32, (BLOCK, BLOCK), 1
    )
    for b in range(STEP // BLOCK):
        tokens = slice(b * BLOCK, (b + 1) * BLOCK)
        cols = wcol[b]
        grown = jnp.exp(cols)
        for at, h in enumerate(heads):
            lanes = slice((h - lane) * DH, (h - lane + 1) * DH)
            q_b, k_b, v_b = q[tokens, lanes], k[tokens, lanes], v[tokens, lanes]
            spread = cols[:, h : h + 1] - wrow[b, h : h + 1]
            mask = jnp.exp(jnp.where(causal, jnp.minimum(spread, 0.0), -1e30))
            scores = (dot(q_b, k_b, ((1,), (1,))) * mask).astype(BF16)
            reached = (q_b.astype(F32) * grown[:, h : h + 1]).astype(BF16)
            carried = prefix[at]
            incoming = (before[b, h - lane] + carried).astype(BF16)
            attended = dot(scores, v_b) + dot(reached, incoming)
            prefix[at] = carried * grown[BLOCK - 1 :, h : h + 1]
            mean = jnp.mean(attended * attended, axis=1, keepdims=True)
            out[tokens, at * DH : (at + 1) * DH] = (attended * lax.rsqrt(mean + 1e-5)).astype(BF16)


def out_kernel(plan, order, lead, features, *rest):
    if lead:
        earlier, rest = rest[0], rest[1:]
    weights, out = rest[:-1], rest[-1]
    mine, place = lax.axis_index("head"), lax.axis_index("seq")
    sources = features.shape[0]
    for offset, pieces in plan:
        total = None
        for at, first, count, lane, row, size, stride in pieces:
            for r in range(first, first + count):
                left = features[lax.bitwise_xor(mine, order[r]), :, lane : lane + size]
                start = (r - first) * stride + row
                term = dot(left, weights[at][start : start + size])
                total = term if total is None else total + term
        width = total.shape[1]
        columns = pl.ds(pl.multiple_of(lax.bitwise_xor(place, offset) * width, width), width)
        if lead:
            total = total + earlier[:, columns]
        out[:, columns] = total.astype(out.dtype)


def params(limit):
    return pltpu.CompilerParams(vmem_limit_bytes=limit, dimension_semantics=("arbitrary",))


def cost(flops, moved):
    return pl.CostEstimate(flops=flops, bytes_accessed=moved, transcendentals=0)


def whole_block(shape):
    return pl.BlockSpec(shape, lambda i: (0,) * len(shape))


def keys_values(activations, w_key, w_value, log_decay):
    tokens, width = activations.shape
    heads = log_decay.shape[0]
    columns, blocks, inner = heads * DH, tokens // BLOCK, STEP // BLOCK
    row_block = pl.BlockSpec((STEP, columns), lambda i: (i, 0))
    return pl.pallas_call(
        kv_kernel,
        grid=(tokens // STEP,),
        in_specs=[
            pl.BlockSpec((STEP, width), lambda i: (i, 0)),
            whole_block((width, columns)),
            whole_block((width, columns)),
            whole_block((heads, tokens)),
        ],
        out_specs=[
            row_block,
            row_block,
            pl.BlockSpec((inner, heads, DH, DH), lambda i: (i, 0, 0, 0)),
            whole_block((heads, DH + EXTRA, DH)),
            whole_block((blocks, BLOCK, 8)),
            whole_block((blocks, 8, BLOCK)),
        ],
        out_shape=[
            jax.ShapeDtypeStruct((tokens, columns), BF16),
            jax.ShapeDtypeStruct((tokens, columns), BF16),
            jax.ShapeDtypeStruct((blocks, heads, DH, DH), F32),
            jax.ShapeDtypeStruct((heads, DH + EXTRA, DH), BF16),
            jax.ShapeDtypeStruct((blocks, BLOCK, 8), F32),
            jax.ShapeDtypeStruct((blocks, 8, BLOCK), F32),
        ],
        scratch_shapes=[pltpu.VMEM((heads, DH, DH), F32), pltpu.VMEM((8, DH), F32)],
        compiler_params=params(60 * MIB),
        cost_estimate=cost(4 * tokens * width * columns, 4 * tokens * width),
        name="keys_values",
    )(activations, w_key, w_value, log_decay)


def queries(activations, w_query):
    tokens, width = activations.shape
    columns = w_query.shape[1]
    return pl.pallas_call(
        project_kernel,
        grid=(tokens // STEP,),
        in_specs=[pl.BlockSpec((STEP, width), lambda i: (i, 0)), whole_block((width, columns))],
        out_specs=pl.BlockSpec((STEP, columns), lambda i: (i, 0)),
        out_shape=jax.ShapeDtypeStruct((tokens, columns), BF16),
        compiler_params=params(60 * MIB),
        cost_estimate=cost(2 * tokens * width * columns, 2 * tokens * width),
        name="queries",
    )(activations, w_query)


def attend(first, count, query, key, value, before, wcol, wrow, arrivals):
    tokens, columns = query.shape
    heads, inner = columns // DH, STEP // BLOCK
    held = count if first % count == 0 else heads
    group = first // held
    row_block = pl.BlockSpec((STEP, held * DH), lambda i: (i, group))
    return pl.pallas_call(
        functools.partial(attend_kernel, first, count, group * held, len(arrivals)),
        grid=(tokens // STEP,),
        in_specs=[
            row_block,
            row_block,
            row_block,
            pl.BlockSpec((inner, held, DH, DH), lambda i: (i, group, 0, 0)),
            pl.BlockSpec((inner, BLOCK, 8), lambda i: (i, 0, 0)),
            pl.BlockSpec((inner, 8, BLOCK), lambda i: (i, 0, 0)),
        ]
        + [whole_block(piece.shape) for piece in arrivals],
        out_specs=pl.BlockSpec((STEP, count * DH), lambda i: (i, 0)),
        out_shape=jax.ShapeDtypeStruct((tokens, count * DH), BF16),
        scratch_shapes=[pltpu.VMEM((count, DH, DH), F32)],
        compiler_params=params(60 * MIB),
        cost_estimate=cost(8 * tokens * BLOCK * count * DH, 8 * tokens * count * DH),
        name="attend",
    )(query, key, value, before, wcol, wrow, *arrivals)


def swap(value, axis, bit):
    count = lax.axis_size(axis)
    return lax.ppermute(value, axis, [(i, i ^ bit) for i in range(count)])


def bits_of(count):
    return [1 << b for b in reversed(range(count.bit_length() - 1))]


def gather_rows(w_out):
    half = w_out.shape[0] // 2
    piece = lax.dynamic_slice_in_dim(w_out, lax.axis_index("grp") * half, half, axis=0)
    return piece, swap(piece, "head", bits_of(lax.axis_size("head"))[0])


def gather_rest(piece, received):
    top, *others = bits_of(lax.axis_size("head"))
    order = [0, top]
    piece = jnp.concatenate([piece, received], axis=0)
    for bit in others[:-1]:
        piece = jnp.concatenate([piece, swap(piece, "head", bit)], axis=0)
        order = order + [r ^ bit for r in order]
    return piece, swap(piece, "head", others[-1]), order + [r ^ others[-1] for r in order]


def gather_columns(piece):
    middle = piece.shape[0] // 2
    across, beside = swap(piece, "seq", 2), swap(piece, "grp", 1)
    corner = [swap(beside[:middle], "seq", 2), swap(across[middle:], "grp", 1)]
    found = {(0, 0): [piece], (0, 2): [across], (1, 0): [beside], (1, 2): corner}
    for bit in bits_of(lax.axis_size("seq"))[:-2]:
        found.update(
            {
                (g, s ^ bit): [swap(part, "seq", bit) for part in parts]
                for (g, s), parts in list(found.items())
            }
        )
    found.update(
        {(g, s ^ 1): [swap(part, "seq", 1) for part in parts] for (g, s), parts in found.items()}
    )
    return found


def project_out(features, found, order, first, count, heads, earlier, dtype):
    sources, rows, _ = features.shape
    half = heads // 2
    operands, plan = [], []
    for offset in sorted({s for _, s in found}):
        pieces = []
        for g in range(2):
            low, high = max(first, g * half), min(first + count, (g + 1) * half)
            if low >= high:
                continue
            done = 0
            for part in found[(g, offset)]:
                held = part.shape[0] // (half * DH)
                pieces.append((len(operands), done, held, (low - first) * DH, (low - g * half) * DH,
                               (high - low) * DH, half * DH))
                operands.append(part)
                done += held
        plan.append((offset, tuple(pieces)))
    width = sum(1 for _ in plan) * operands[0].shape[1]
    lead = [] if earlier is None else [earlier]
    return pl.pallas_call(
        functools.partial(out_kernel, tuple(plan), order, bool(lead)),
        out_shape=jax.ShapeDtypeStruct((rows, width), dtype),
        compiler_params=pltpu.CompilerParams(vmem_limit_bytes=60 * MIB),
        cost_estimate=cost(2 * rows * width * sources * count * DH, 4 * width * sources * count * DH),
        name="project_out",
    )(features, *lead, *operands)


def after(value, *earlier):
    return lax.optimization_barrier((value, *earlier))[0]


def on_device(activations, w_query, w_key, w_value, w_out, log_decay):
    heads, tokens = log_decay.shape
    places, sources = lax.axis_size("seq"), lax.axis_size("head")
    own, farthest = gather_rows(w_out)
    key, value, before, payload, wcol, wrow = keys_values(activations, w_key, w_value, log_decay)
    payload, farthest = lax.optimization_barrier((payload, farthest))
    arrivals = [
        lax.ppermute(payload, "seq", [(i, i + r) for i in range(places - r)])
        for r in range(1, places)
    ]
    low, high, order = gather_rest(own, farthest)
    query = queries(after(activations, low), w_query)
    chunks = CHUNKS if heads == 4 else ((0, heads),)
    query, high = lax.optimization_barrier((query, high))
    sends = []
    for first, last in chunks:
        normed = attend(first, last - first, query, key, value, before, wcol, wrow, arrivals)
        if not sends:
            high = after(high, normed)
        sends.append(
            lax.all_to_all(
                normed.reshape(sources, tokens // sources, (last - first) * DH), "head", 0, 0
            )
        )
    found = gather_columns(jnp.concatenate([low, high], axis=0))
    mixed = None
    for (first, last), features in zip(chunks, sends):
        dtype = BF16 if last == heads else F32
        mixed = project_out(features, found, order, first, last - first, heads, mixed, dtype)
    return mixed


def solution(mesh):
    return jax.shard_map(
        on_device,
        mesh=mesh,
        in_specs=(
            P(("grp", "seq"), None),
            P(None, "head"),
            P(None, "head"),
            P(None, "head"),
            P("head", "seq"),
            P("head", ("grp", "seq")),
        ),
        out_specs=P(("grp", "seq", "head"), None),
        check_vma=False,
    )
```

```python
import functools

import jax
import jax.numpy as jnp
from jax import lax
from jax.experimental import pallas as pl
from jax.experimental.pallas import tpu as pltpu
from jax.sharding import PartitionSpec as P

DH = 128
BLOCK = 256
STEP = 512
EXTRA = 16
F32 = jnp.float32
BF16 = jnp.bfloat16
HIGHEST = lax.Precision.HIGHEST
MIB = 1 << 20


def dot(a, b, dims=((1,), (0,)), precision=None):
    return lax.dot_general(a, b, (dims, ((), ())), precision=precision, preferred_element_type=F32)


def relative_half(part, width):
    start = lax.rem(part + lax.axis_index("grp"), 2) * width
    return pl.ds(pl.multiple_of(start, width), width)


def kv_kernel(act, wk, wv, wq, decay, act_out, wq_out, kv_out, before, payload, wcol, wrow, reach,
              held, logs, state, sems):
    heads, tokens = decay.shape
    blocks, steps = tokens // BLOCK, tokens // STEP
    half = heads // 2
    wide = half * DH
    columns = heads * DH

    def load_rows(step):
        rows = pl.ds(pl.multiple_of(step * STEP, STEP), STEP)
        return pltpu.make_async_copy(act.at[rows], act_out.at[rows], sems.at[step])

    def load_half(source, target, part, lane, at):
        return pltpu.make_async_copy(
            source.at[:, relative_half(part, wide)],
            target.at[:, pl.ds(lane, wide)],
            sems.at[steps + at],
        )

    load_logs = pltpu.make_async_copy(decay, logs, sems.at[steps + 6])
    weights = [
        load_half(source, held, part, at * wide, at)
        for at, (source, part) in enumerate([(wk, 0), (wk, 1), (wv, 0), (wv, 1)])
    ]
    q_loads = [load_half(wq, wq_out, part, part * wide, 4 + part) for part in range(2)]
    queue = [load_rows(0)] + weights + [load_rows(1)]
    for copy in [load_logs] + queue[:3]:
        copy.start()

    load_logs.wait()
    rates = logs[...]
    swapped = jnp.concatenate([rates[half:], rates[:half]], axis=0)
    rates = jnp.where(lax.axis_index("grp") == 0, rates, swapped)
    rates = jnp.concatenate([rates, jnp.zeros((8 - heads, tokens), F32)], axis=0)
    stacked = jnp.concatenate([rates[:, n * BLOCK : (n + 1) * BLOCK] for n in range(blocks)], axis=0)
    upper = (
        lax.broadcasted_iota(jnp.int32, (BLOCK, BLOCK), 0)
        <= lax.broadcasted_iota(jnp.int32, (BLOCK, BLOCK), 1)
    ).astype(F32)
    within = dot(stacked, upper, precision=HIGHEST)
    total = jnp.zeros((8, 1), F32)
    for n in range(blocks):
        rows = within[n * 8 : (n + 1) * 8]
        wrow[n] = rows
        wcol[n] = rows.T
        reach[n] = jnp.broadcast_to(jnp.exp(total), (8, DH))
        total = total + rows[:, BLOCK - 1 :]
    factor = jnp.broadcast_to(jnp.exp(total), (8, DH))
    state[...] = jnp.zeros_like(state)

    def advance(step, first):
        start = pl.multiple_of(step * STEP, STEP)
        rows = pl.ds(start, STEP)
        if first:
            for at in range(5):
                queue[at].wait()
                if at + 3 < len(queue):
                    queue[at + 3].start()
                if at > 0:
                    lanes = slice((at - 1) * wide, at * wide)
                    kv_out[rows, lanes] = dot(act_out[rows], held[:, lanes]).astype(BF16)
        else:
            load_rows(step).wait()

            @pl.when(step + 1 < steps)
            def _():
                load_rows(step + 1).start()

            kv_out[rows] = dot(act_out[rows], held[...]).astype(BF16)
        for b in range(STEP // BLOCK):
            n = step * (STEP // BLOCK) + b
            cols = wcol[n]
            last = cols[BLOCK - 1 :]
            carry = jnp.exp(last - cols)
            shrink = jnp.exp(last)
            block = pl.ds(pl.multiple_of(start + b * BLOCK, BLOCK), BLOCK)
            for h in range(heads):
                k_b = kv_out[block, h * DH : (h + 1) * DH].astype(F32) * carry[:, h : h + 1]
                v_b = kv_out[block, columns + h * DH : columns + (h + 1) * DH]
                update = dot(k_b.astype(BF16), v_b, ((0,), (0,)))
                old = state[h]
                before[n, h] = old
                state[h] = shrink[:, h : h + 1] * old + update

    advance(0, True)
    for copy in q_loads:
        copy.start()

    @pl.loop(1, steps)
    def _(step):
        advance(step, False)

    for h in range(heads):
        payload[h, :DH] = state[h].astype(BF16)
        whole = jnp.broadcast_to(factor[h : h + 1], (EXTRA, DH))
        high = whole.astype(BF16).astype(F32)
        first = lax.broadcasted_iota(jnp.int32, (EXTRA, DH), 0) < EXTRA // 2
        payload[h, DH:] = jnp.where(first, high, whole - high).astype(BF16)
    for copy in q_loads:
        copy.wait()


def project_kernel(act, w, out):
    for step in range(act.shape[0] // STEP):
        rows = pl.ds(step * STEP, STEP)
        out[rows] = dot(act[rows], w[...]).astype(BF16)


def incoming_state(arrivals, h):
    place = lax.axis_index("seq")
    sources = [lax.bitwise_xor(place, r + 1) for r in range(len(arrivals))]
    reaches = []
    for piece in arrivals:
        extra = piece[h, DH:].astype(F32)
        reaches.append(extra[:1] + extra[EXTRA // 2 : EXTRA // 2 + 1])
    total = jnp.zeros((DH, DH), F32)
    for source, piece in zip(sources, arrivals):
        weight = jnp.where(source < place, jnp.ones((1, DH), F32), 0.0)
        for other, reach in zip(sources, reaches):
            between = jnp.logical_and(other > source, other < place)
            weight = weight * jnp.where(between, reach, 1.0)
        total = total + weight * piece[h, :DH].astype(F32)
    return total


def attend_kernel(received, q, kv, before, wcol, wrow, reach, *rest):
    arrivals, (out, held, sems) = rest[:received], rest[received:]
    sources, share, columns = out.shape
    heads = columns // DH

    def send(target):
        return pltpu.make_async_copy(held.at[target], out.at[target], sems.at[target])

    causal = lax.broadcasted_iota(jnp.int32, (BLOCK, BLOCK), 0) >= lax.broadcasted_iota(
        jnp.int32, (BLOCK, BLOCK), 1
    )
    prefix = [incoming_state(arrivals, h) for h in range(heads)]

    @pl.loop(0, sources)
    def _(target):
        for b in range(share // BLOCK):
            n = target * (share // BLOCK) + b
            rows = pl.ds(pl.multiple_of(n * BLOCK, BLOCK), BLOCK)
            cols = wcol[n]
            grown = jnp.exp(cols)
            reached_here = reach[n]
            for h in range(heads):
                lanes = slice(h * DH, (h + 1) * DH)
                q_b, k_b = q[rows, lanes], kv[rows, lanes]
                v_b = kv[rows, columns + h * DH : columns + (h + 1) * DH]
                spread = cols[:, h : h + 1] - wrow[n, h : h + 1]
                mask = jnp.exp(jnp.where(causal, jnp.minimum(spread, 0.0), -1e30))
                scores = (dot(q_b, k_b, ((1,), (1,))) * mask).astype(BF16)
                reached = (q_b.astype(F32) * grown[:, h : h + 1]).astype(BF16)
                incoming = (before[n, h] + reached_here[h : h + 1] * prefix[h]).astype(BF16)
                attended = dot(scores, v_b) + dot(reached, incoming)
                mean = jnp.mean(attended * attended, axis=1, keepdims=True)
                normed = (attended * lax.rsqrt(mean + 1e-5)).astype(BF16)
                held[target, b * BLOCK : (b + 1) * BLOCK, lanes] = normed
        send(target).start()

    for target in range(sources):
        send(target).wait()


def out_kernel(plan, features, *rest):
    weights, (out, held, sems) = rest[:-3], rest[-3:]
    mine, place = lax.axis_index("head"), lax.axis_index("seq")
    half = features.shape[2] // 2

    def load(slot, at, begin):
        rows = weights[at].shape[0]
        return pltpu.make_async_copy(weights[at], held.at[slot, pl.ds(begin, rows)], sems.at[at])

    def loads(at):
        offset, pieces, products = plan[at]
        return [load(at, piece, begin) for piece, begin in pieces]

    for at in range(len(plan)):
        if at < 2:
            for copy in loads(at):
                copy.start()
    for at, (offset, pieces, products) in enumerate(plan):
        for copy in loads(at):
            copy.wait()
        if at + 2 < len(plan):
            for copy in loads(at + 2):
                copy.start()
        total = None
        for source, lane, row in products:
            left = features[lax.bitwise_xor(mine, source), :, lane : lane + half]
            term = dot(left, held[at, row : row + half])
            total = term if total is None else total + term
        width = total.shape[1]
        columns = pl.ds(pl.multiple_of(lax.bitwise_xor(place, offset) * width, width), width)
        out[:, columns] = total.astype(out.dtype)


def cost(flops, moved):
    return pl.CostEstimate(flops=flops, bytes_accessed=moved, transcendentals=0)


def in_hbm():
    return pl.BlockSpec(memory_space=pltpu.HBM)


def stay_in_hbm(*values):
    return [pltpu.with_memory_space_constraint(value, pltpu.HBM) for value in values]


def in_vmem():
    return pl.BlockSpec(memory_space=pltpu.VMEM)


def keys_values(activations, w_key, w_value, w_query, log_decay):
    tokens, width = activations.shape
    heads = log_decay.shape[0]
    columns, blocks = heads * DH, tokens // BLOCK
    shapes = [
        ((tokens, width), BF16),
        ((width, columns), BF16),
        ((tokens, 2 * columns), BF16),
        ((blocks, heads, DH, DH), F32),
        ((heads, DH + EXTRA, DH), BF16),
        ((blocks, BLOCK, 8), F32),
        ((blocks, 8, BLOCK), F32),
        ((blocks, 8, DH), F32),
    ]
    return pl.pallas_call(
        kv_kernel,
        in_specs=[in_hbm()] * 5,
        out_specs=[in_vmem()] * len(shapes),
        out_shape=[pltpu.VMEM(*shape) for shape in shapes],
        scratch_shapes=[
            pltpu.VMEM((width, 2 * columns), BF16),
            pltpu.VMEM((heads, tokens), F32),
            pltpu.VMEM((heads, DH, DH), F32),
            pltpu.SemaphoreType.DMA((tokens // STEP + 7,)),
        ],
        compiler_params=pltpu.CompilerParams(vmem_limit_bytes=16 * MIB),
        cost_estimate=cost(4 * tokens * width * columns, 4 * tokens * width),
        name="keys_values",
    )(*stay_in_hbm(activations, w_key, w_value, w_query, log_decay))


def queries(activations, w_query):
    tokens, width = activations.shape
    columns = w_query.shape[1]
    return pl.pallas_call(
        project_kernel,
        in_specs=[in_vmem()] * 2,
        out_specs=in_vmem(),
        out_shape=pltpu.VMEM((tokens, columns), BF16),
        compiler_params=pltpu.CompilerParams(vmem_limit_bytes=16 * MIB),
        cost_estimate=cost(2 * tokens * width * columns, 2 * tokens * width),
        name="queries",
    )(activations, w_query)


def attend(sources, query, *rest):
    received = len(rest) - 5
    tokens, columns = query.shape
    shares = (sources, tokens // sources, columns)
    return pl.pallas_call(
        functools.partial(attend_kernel, received),
        in_specs=[in_vmem()] * (len(rest) + 1),
        out_specs=in_hbm(),
        out_shape=pltpu.HBM(shares, BF16),
        scratch_shapes=[pltpu.VMEM(shares, BF16), pltpu.SemaphoreType.DMA((sources,))],
        compiler_params=pltpu.CompilerParams(vmem_limit_bytes=16 * MIB),
        cost_estimate=cost(20 * tokens * BLOCK * columns, 8 * tokens * columns),
        name="attend",
    )(query, *rest)


def swap(value, axis, bit):
    count = lax.axis_size(axis)
    return lax.ppermute(value, axis, [(i, i ^ bit) for i in range(count)])


def bits_of(count):
    return [1 << b for b in reversed(range(count.bit_length() - 1))]


def gather_rows(w_out):
    half = w_out.shape[0] // 2
    piece = lax.dynamic_slice_in_dim(w_out, lax.axis_index("grp") * half, half, axis=0)
    return piece, swap(piece, "head", bits_of(lax.axis_size("head"))[0])


def gather_rest(piece, received):
    top, *others = bits_of(lax.axis_size("head"))
    order = [0, top]
    piece = jnp.concatenate([piece, received], axis=0)
    for bit in others[:-1]:
        piece = jnp.concatenate([piece, swap(piece, "head", bit)], axis=0)
        order = order + [r ^ bit for r in order]
    return piece, swap(piece, "head", others[-1]), order + [r ^ others[-1] for r in order]


def gather_columns(piece):
    middle = piece.shape[0] // 2
    across, beside = swap(piece, "seq", 2), swap(piece, "grp", 1)
    corner = [swap(beside[:middle], "seq", 2), swap(across[middle:], "grp", 1)]
    found = {(0, 0): [piece], (0, 2): [across], (1, 0): [beside], (1, 2): corner}
    for bit in bits_of(lax.axis_size("seq"))[:-2]:
        found.update(
            {
                (g, s ^ bit): [swap(part, "seq", bit) for part in parts]
                for (g, s), parts in list(found.items())
            }
        )
    found.update(
        {(g, s ^ 1): [swap(part, "seq", 1) for part in parts] for (g, s), parts in found.items()}
    )
    return found


def project_out(features, found, order):
    sources, rows, columns = features.shape
    half = columns // 2
    operands, plan = [], []
    for offset in sorted({s for _, s in found}):
        pieces, products, begin = [], [], 0
        for g in range(2):
            for r in order:
                products.append((r, g * half, begin + order.index(r) * half))
            for part in found[(g, offset)]:
                pieces.append((len(operands), begin))
                operands.append(part)
                begin += part.shape[0]
        plan.append((offset, tuple(pieces), tuple(products)))
    width = operands[0].shape[1]
    return pl.pallas_call(
        functools.partial(out_kernel, tuple(plan)),
        out_shape=jax.ShapeDtypeStruct((rows, len(plan) * width), BF16),
        in_specs=[in_vmem()] + [in_hbm()] * len(operands),
        out_specs=in_vmem(),
        scratch_shapes=[
            pltpu.VMEM((len(plan), sources * columns, width), BF16),
            pltpu.SemaphoreType.DMA((len(operands),)),
        ],
        compiler_params=pltpu.CompilerParams(vmem_limit_bytes=24 * MIB),
        cost_estimate=cost(2 * rows * sources * columns * width * len(plan), 8 * MIB),
        name="project_out",
    )(features, *stay_in_hbm(*operands))


def after(value, *earlier):
    return lax.optimization_barrier((value, *earlier))[0]


def on_device(activations, w_query, w_key, w_value, w_out, log_decay):
    heads, tokens = log_decay.shape
    places, sources = lax.axis_size("seq"), lax.axis_size("head")
    own, farthest = gather_rows(w_out)
    rows, w_query, kv, before, payload, wcol, wrow, reach = keys_values(
        activations, w_key, w_value, w_query, log_decay
    )
    payload, farthest = lax.optimization_barrier((payload, farthest))
    arrivals = [swap(payload, "seq", r) for r in range(1, places)]
    low, high, order = gather_rest(own, farthest)
    query = queries(after(rows, low), w_query)
    normed = attend(sources, query, kv, before, wcol, wrow, reach, *arrivals)
    normed, high = lax.optimization_barrier((normed, high))
    features = lax.all_to_all(normed, "head", 0, 0)
    found = gather_columns(jnp.concatenate([low, high], axis=0))
    return project_out(features, found, order)


def solution(mesh):
    return jax.shard_map(
        on_device,
        mesh=mesh,
        in_specs=(
            P(("grp", "seq"), None),
            P(None, "head"),
            P(None, "head"),
            P(None, "head"),
            P("head", "seq"),
            P("head", ("grp", "seq")),
        ),
        out_specs=P(("grp", "seq", "head"), None),
        check_vma=False,
    )
```

```python
import functools

import jax
import jax.numpy as jnp
from jax import lax
from jax.experimental import pallas as pl
from jax.experimental.pallas import tpu as pltpu
from jax.sharding import PartitionSpec as P

DH = 128
BLOCK = 256
STEP = 512
AHEAD = 3
OUT_AHEAD = 8
EXTRA = 16
F32 = jnp.float32
BF16 = jnp.bfloat16
HIGHEST = lax.Precision.HIGHEST
LOG2E = 1.4426950408889634
MIB = 1 << 20


def dot(a, b, dims=((1,), (0,)), precision=None):
    return lax.dot_general(a, b, (dims, ((), ())), precision=precision, preferred_element_type=F32)


def relative_half(part, width):
    start = lax.rem(part + lax.axis_index("grp"), 2) * width
    return pl.ds(pl.multiple_of(start, width), width)


def kv_kernel(part, act, wk, wv, wq, decay, act_out, wq_out, kv_out, before, payload, spread, wrow, reach,
              held, logs, state, wcol, sems):
    half, tokens = decay.shape[0] // 2, decay.shape[1]
    blocks = tokens // BLOCK
    wide = half * DH
    chunks = [(0, BLOCK), (BLOCK, STEP - BLOCK)]
    chunks += [(start, STEP) for start in range(STEP, tokens, STEP)]

    def load_rows(start, size):
        rows = pl.ds(start, size)
        return functools.partial(pltpu.make_async_copy, act.at[rows], act_out.at[rows])

    def load_half(source, target, lane):
        return functools.partial(
            pltpu.make_async_copy,
            source.at[:, relative_half(part, wide)],
            target.at[:, pl.ds(lane, wide)],
        )

    matrices = [wk, wv]
    loads = [load_rows(*chunks[0])]
    loads += [load_half(w, held, at * wide) for at, w in enumerate(matrices)]
    loads += [load_rows(*chunk) for chunk in chunks[1:]]
    loads += [load_half(wq, wq_out, 0)]
    queue = [load(sems.at[at]) for at, load in enumerate(loads)]
    load_logs = pltpu.make_async_copy(decay, logs, sems.at[len(queue)])
    load_logs.start()
    for copy in queue[:AHEAD]:
        copy.start()

    def take(at):
        queue[at].wait()
        if at + AHEAD < len(queue):
            queue[at + AHEAD].start()

    load_logs.wait()
    rates = jnp.where(lax.axis_index("grp") == part, logs[:half], logs[half:])
    rates = jnp.concatenate([rates, jnp.zeros((8 - half, tokens), F32)], axis=0)
    stacked = jnp.concatenate([rates[:, n * BLOCK : (n + 1) * BLOCK] for n in range(blocks)], axis=0)
    upper = (
        lax.broadcasted_iota(jnp.int32, (BLOCK, BLOCK), 0)
        <= lax.broadcasted_iota(jnp.int32, (BLOCK, BLOCK), 1)
    ).astype(F32)
    within = LOG2E * dot(stacked, upper, precision=HIGHEST)
    total = jnp.zeros((8, 1), F32)
    for n in range(blocks):
        rows = within[n * 8 : (n + 1) * 8]
        wrow[n] = rows
        wcol[n] = rows.T
        reach[n] = jnp.broadcast_to(jnp.exp2(total), (8, DH))
        total = total + rows[:, BLOCK - 1 :]
    factor = jnp.broadcast_to(jnp.exp2(total), (8, DH))
    state[...] = jnp.zeros_like(state)

    for chunk, (start, size) in enumerate(chunks):
        rows = slice(start, start + size)
        take(chunk + len(matrices) if chunk else 0)
        halves = []
        for at in range(len(matrices)):
            if chunk == 0:
                take(1 + at)
            lanes = slice(at * wide, (at + 1) * wide)
            halves.append(dot(act_out[rows], held[:, lanes]).astype(BF16))
            kv_out[rows, lanes] = halves[at]
        for b in range(size // BLOCK):
            n = start // BLOCK + b
            block = slice(b * BLOCK, (b + 1) * BLOCK)
            for h in range(half):
                lanes = slice(h * DH, (h + 1) * DH)
                cols = jnp.broadcast_to(wcol[n][:, h : h + 1], (BLOCK, DH))
                spread[n, h] = cols
                last = cols[BLOCK - 1 :]
                k_b = halves[0][block, lanes].astype(F32) * jnp.exp2(last - cols)
                update = dot(k_b.astype(BF16), halves[1][block, lanes], ((0,), (0,)))
                old = state[h]
                before[n, h] = old
                state[h] = jnp.exp2(last) * old + update

    for h in range(half):
        payload[h, :DH] = state[h].astype(BF16)
        whole = jnp.broadcast_to(factor[h : h + 1], (EXTRA, DH))
        high = whole.astype(BF16).astype(F32)
        first = lax.broadcasted_iota(jnp.int32, (EXTRA, DH), 0) < EXTRA // 2
        payload[h, DH:] = jnp.where(first, high, whole - high).astype(BF16)
    take(len(queue) - 1)


def project_kernel(act, w, out):
    for step in range(act.shape[0] // STEP):
        rows = slice(step * STEP, (step + 1) * STEP)
        out[rows] = dot(act[rows], w[...]).astype(BF16)


def incoming_state(arrivals, h):
    place = lax.axis_index("seq")
    sources = [lax.bitwise_xor(place, r + 1) for r in range(len(arrivals))]
    reaches = []
    for piece in arrivals:
        extra = piece[h, DH:].astype(F32)
        reaches.append(extra[:1] + extra[EXTRA // 2 : EXTRA // 2 + 1])
    total = jnp.zeros((DH, DH), F32)
    for source, piece in zip(sources, arrivals):
        weight = jnp.where(source < place, jnp.ones((1, DH), F32), 0.0)
        for other, reach in zip(sources, reaches):
            between = jnp.logical_and(other > source, other < place)
            weight = weight * jnp.where(between, reach, 1.0)
        total = total + weight * piece[h, :DH].astype(F32)
    return total


def attend_kernel(received, q, kv, before, spread, wrow, reach, *rest):
    arrivals, (out, held, bound, sems) = rest[:received], rest[received:]
    sources, share, columns = out.shape
    heads = columns // DH

    def send(target):
        return pltpu.make_async_copy(held.at[target], out.at[target], sems.at[target])

    causal = lax.broadcasted_iota(jnp.int32, (BLOCK, BLOCK), 0) >= lax.broadcasted_iota(
        jnp.int32, (BLOCK, BLOCK), 1
    )
    bound[...] = jnp.where(causal, 0.0, -1e30)
    prefix = [incoming_state(arrivals, h) for h in range(heads)]

    @pl.loop(0, sources)
    def _(target):
        for b in range(share // BLOCK):
            n = target * (share // BLOCK) + b
            rows = pl.ds(pl.multiple_of(n * BLOCK, BLOCK), BLOCK)
            reached = reach[n]
            lanes = [slice(h * DH, (h + 1) * DH) for h in range(heads)]
            scores = [dot(q[rows, lane], kv[rows, lane], ((1,), (1,))) for lane in lanes]
            carried = []
            for h, lane in enumerate(lanes):
                incoming = (before[n, h] + reached[h : h + 1] * prefix[h]).astype(BF16)
                carried.append(dot(q[rows, lane], incoming))
            weights = []
            for h in range(heads):
                cols = spread[n, h]
                gap = jnp.concatenate([cols] * (BLOCK // DH), axis=1) - wrow[n, h : h + 1]
                weights.append((scores[h] * jnp.exp2(jnp.minimum(gap, bound[...]))).astype(BF16))
            for h, lane in enumerate(lanes):
                v_b = kv[rows, columns + h * DH : columns + (h + 1) * DH]
                attended = dot(weights[h], v_b) + jnp.exp2(spread[n, h]) * carried[h]
                mean = jnp.mean(attended * attended, axis=1, keepdims=True)
                normed = (attended * lax.rsqrt(mean + 1e-5)).astype(BF16)
                held[target, b * BLOCK : (b + 1) * BLOCK, lane] = normed
        send(target).start()

    for target in range(sources):
        send(target).wait()


def out_kernel(offsets, order, begun, features, *rest):
    if begun:
        earlier, rest = rest[0], rest[1:]
    weights, (out, left, held, ready, done, sems, out_sems) = rest[:-7], rest[-7:]
    mine, place = lax.axis_index("head"), lax.axis_index("seq")
    half = features.shape[2]
    width = done.shape[2]
    each = len(weights) // len(offsets)

    def store(slot):
        if not begun:
            return pltpu.make_async_copy(done.at[slot], out.at[slot], out_sems.at[slot])
        columns = pl.ds(pl.multiple_of(lax.bitwise_xor(place, offsets[slot]) * width, width), width)
        return pltpu.make_async_copy(done.at[slot], out.at[:, columns], out_sems.at[slot])

    loads, parts = [], []
    for slot in range(len(offsets)):
        begin = 0
        for piece in weights[slot * each : (slot + 1) * each]:
            rows = pl.ds(begin, piece.shape[0])
            parts.append((slot, rows, len(loads)))
            loads.append((piece, held.at[slot, rows]))
            begin += piece.shape[0]
        if begun:
            loads.append((earlier.at[slot], ready.at[slot]))
    queue = [pltpu.make_async_copy(*pair, sems.at[i]) for i, pair in enumerate(loads)]
    for copy in queue[:OUT_AHEAD]:
        copy.start()

    def take(i):
        queue[i].wait()
        if i + OUT_AHEAD < len(queue):
            queue[i + OUT_AHEAD].start()

    for i, r in enumerate(order):
        left[:, i * half : (i + 1) * half] = features[lax.bitwise_xor(mine, r)]
    for slot in range(len(offsets)):
        total = None
        for at, rows, i in parts:
            if at == slot:
                take(i)
                term = dot(left[:, rows], held[slot, rows])
                total = term if total is None else total + term
        if begun:
            take((slot + 1) * (each + 1) - 1)
            total = total + ready[slot]
        done[slot] = total.astype(done.dtype)
        store(slot).start()
    for slot in range(len(offsets)):
        store(slot).wait()


def cost(flops, moved):
    return pl.CostEstimate(flops=flops, bytes_accessed=moved, transcendentals=0)


def in_hbm():
    return pl.BlockSpec(memory_space=pltpu.HBM)


def stay_in_hbm(*values):
    return [pltpu.with_memory_space_constraint(value, pltpu.HBM) for value in values]


def in_vmem():
    return pl.BlockSpec(memory_space=pltpu.VMEM)


def keys_values(part, activations, w_key, w_value, w_query, log_decay):
    tokens, width = activations.shape
    heads = log_decay.shape[0] // 2
    columns, blocks = heads * DH, tokens // BLOCK
    shapes = [
        ((tokens, width), BF16),
        ((width, columns), BF16),
        ((tokens, 2 * columns), BF16),
        ((blocks, heads, DH, DH), F32),
        ((heads, DH + EXTRA, DH), BF16),
        ((blocks, heads, BLOCK, DH), F32),
        ((blocks, 8, BLOCK), F32),
        ((blocks, 8, DH), F32),
    ]
    return pl.pallas_call(
        functools.partial(kv_kernel, part),
        in_specs=[in_hbm()] * 5,
        out_specs=[in_vmem()] * len(shapes),
        out_shape=[pltpu.VMEM(*shape) for shape in shapes],
        scratch_shapes=[
            pltpu.VMEM((width, 2 * columns), BF16),
            pltpu.VMEM((2 * heads, tokens), F32),
            pltpu.VMEM((heads, DH, DH), F32),
            pltpu.VMEM((blocks, BLOCK, 8), F32),
            pltpu.SemaphoreType.DMA((tokens // STEP + 8,)),
        ],
        compiler_params=pltpu.CompilerParams(vmem_limit_bytes=16 * MIB),
        cost_estimate=cost(4 * tokens * width * columns, 4 * tokens * width),
        name="keys_values",
    )(*stay_in_hbm(activations, w_key, w_value, w_query, log_decay))


def queries(activations, w_query):
    tokens, width = activations.shape
    columns = w_query.shape[1]
    return pl.pallas_call(
        project_kernel,
        in_specs=[in_vmem()] * 2,
        out_specs=in_vmem(),
        out_shape=pltpu.VMEM((tokens, columns), BF16),
        compiler_params=pltpu.CompilerParams(vmem_limit_bytes=16 * MIB),
        cost_estimate=cost(2 * tokens * width * columns, 2 * tokens * width),
        name="queries",
    )(activations, w_query)


def attend(sources, query, *rest):
    received = len(rest) - 5
    tokens, columns = query.shape
    shares = (sources, tokens // sources, columns)
    return pl.pallas_call(
        functools.partial(attend_kernel, received),
        in_specs=[in_vmem()] * (len(rest) + 1),
        out_specs=in_hbm(),
        out_shape=pltpu.HBM(shares, BF16),
        scratch_shapes=[
            pltpu.VMEM(shares, BF16),
            pltpu.VMEM((BLOCK, BLOCK), F32),
            pltpu.SemaphoreType.DMA((sources,)),
        ],
        compiler_params=pltpu.CompilerParams(vmem_limit_bytes=16 * MIB),
        cost_estimate=cost(20 * tokens * BLOCK * columns, 8 * tokens * columns),
        name="attend",
    )(query, *rest)


def swap(value, axis, bit):
    count = lax.axis_size(axis)
    return lax.ppermute(value, axis, [(i, i ^ bit) for i in range(count)])


def bits_of(count):
    return [1 << b for b in reversed(range(count.bit_length() - 1))]


def gather_rows(w_out):
    half = w_out.shape[0] // 2
    own = lax.dynamic_slice_in_dim(w_out, lax.axis_index("grp") * half, half, axis=0)
    return {0: own} | {bit: swap(own, "head", bit) for bit in bits_of(lax.axis_size("head"))}


def gather_rest(pieces):
    pieces = dict(pieces)
    for r in range(lax.axis_size("head")):
        if r not in pieces:
            pieces[r] = swap(pieces[r & (r - 1)], "head", r & -r)
    return pieces


def gather_columns(even, odd, even_across, even_beside, settled):
    across, beside = [even_across], [even_beside]
    even_beside, odd = after((even_beside, odd), *settled)
    odd_across, odd_beside = lax.optimization_barrier((swap(odd, "seq", 2), swap(odd, "grp", 1)))
    across.append(odd_across)
    beside.append(odd_beside)
    corner = [swap(even_beside, "seq", 2), swap(across[1], "grp", 1)]
    found = {(0, 0): [even, odd], (0, 2): across, (1, 0): beside, (1, 2): corner}
    for bit in bits_of(lax.axis_size("seq"))[:-2]:
        found.update(
            {
                (g, s ^ bit): [swap(part, "seq", bit) for part in parts]
                for (g, s), parts in list(found.items())
            }
        )
    return found


def gather_partner(found):
    return found | {
        (g, s ^ 1): [swap(part, "seq", 1) for part in parts] for (g, s), parts in found.items()
    }


def project_out(features, part, found, order, earlier=None):
    sources, rows, columns = features.shape
    offsets = sorted({s for _, s in found})
    operands = [piece for offset in offsets for piece in found[(part, offset)]]
    width, blocks = operands[0].shape[1], len(offsets)
    lead = [] if earlier is None else [earlier]
    shape = (rows, blocks * width) if lead else (blocks, rows, width)
    dtype = BF16 if lead else F32
    return pl.pallas_call(
        functools.partial(out_kernel, offsets, order, bool(lead)),
        out_shape=pltpu.HBM(shape, dtype),
        in_specs=[in_vmem()] + [in_hbm()] * (len(lead) + len(operands)),
        out_specs=in_hbm(),
        scratch_shapes=[
            pltpu.VMEM((rows, sources * columns), BF16),
            pltpu.VMEM((blocks, sources * columns, width), BF16),
            pltpu.VMEM((blocks, rows, width) if lead else (8, 128), F32),
            pltpu.VMEM((blocks, rows, width), dtype),
            pltpu.SemaphoreType.DMA((len(operands) + blocks * len(lead),)),
            pltpu.SemaphoreType.DMA((blocks,)),
        ],
        compiler_params=pltpu.CompilerParams(vmem_limit_bytes=24 * MIB),
        cost_estimate=cost(2 * rows * sources * columns * width * blocks, 8 * MIB),
        name="project_out",
    )(features, *stay_in_hbm(*lead, *operands))


def after(value, *earlier):
    return lax.optimization_barrier((value, *earlier))[0]


def on_device(activations, w_query, w_key, w_value, w_out, log_decay):
    places, sources = lax.axis_size("seq"), lax.axis_size("head")
    pieces = gather_rows(w_out)
    features = []
    for part in range(2):
        rows, w_part, kv, before, payload, spread, wrow, reach = keys_values(
            part, activations, w_key, w_value, w_query, log_decay
        )
        arrivals = [swap(payload, "seq", r) for r in range(1, places)]
        if part == 0:
            rows, pieces = lax.optimization_barrier((rows, pieces))
            pieces = gather_rest(pieces)
        else:
            rows, across, beside = lax.optimization_barrier((rows, across, beside))
        query = queries(rows, w_part)
        normed = attend(sources, query, kv, before, spread, wrow, reach, *arrivals)
        if part == 0:
            normed, pieces, activations = lax.optimization_barrier((normed, pieces, activations))
            even, odd = [r for r in pieces if r % 2 == 0], [r for r in pieces if r % 2]
            order = even + odd
            even, odd = [
                jnp.concatenate([pieces[r] for r in group], axis=0) for group in (even, odd)
            ]
            across, beside = swap(even, "seq", 2), swap(even, "grp", 1)
        features.append(lax.all_to_all(normed, "head", 0, 0))
    found = gather_columns(even, odd, across, beside, arrivals)
    first = {(g, s): parts for (g, s), parts in found.items() if g == 0}
    begun = project_out(features[0], 0, gather_partner(first), order)
    second = {(g, s): parts for (g, s), parts in found.items() if g == 1}
    second, begun = lax.optimization_barrier((second, begun))
    return project_out(features[1], 1, gather_partner(second), order, begun)


def solution(mesh):
    return jax.shard_map(
        on_device,
        mesh=mesh,
        in_specs=(
            P(("grp", "seq"), None),
            P(None, "head"),
            P(None, "head"),
            P(None, "head"),
            P("head", "seq"),
            P("head", ("grp", "seq")),
        ),
        out_specs=P(("grp", "seq", "head"), None),
        check_vma=False,
    )
```

```python
import functools

import jax
import jax.numpy as jnp
from jax import lax
from jax.experimental import pallas as pl
from jax.experimental.pallas import tpu as pltpu
from jax.sharding import PartitionSpec as P

DH = 128
BLOCK = 256
STEP = 512
AHEAD = 3
OUT_AHEAD = 8
EXTRA = 16
F32 = jnp.float32
BF16 = jnp.bfloat16
HIGHEST = lax.Precision.HIGHEST
LOG2E = 1.4426950408889634
MIB = 1 << 20


def dot(a, b, dims=((1,), (0,)), precision=None):
    return lax.dot_general(a, b, (dims, ((), ())), precision=precision, preferred_element_type=F32)


def relative_half(part, width):
    start = lax.rem(part + lax.axis_index("grp"), 2) * width
    return pl.ds(pl.multiple_of(start, width), width)


def kv_kernel(part, act, wk, wv, wq, decay, act_out, wq_out, kv_out, before, payload, spread, wrow, reach,
              held, logs, state, wcol, sems):
    half, tokens = decay.shape[0] // 2, decay.shape[1]
    blocks = tokens // BLOCK
    wide = half * DH
    chunks = [(0, BLOCK)]
    while sum(chunks[-1]) < tokens:
        start = sum(chunks[-1])
        chunks.append((start, min(start, tokens - start)))

    def load_rows(start, size):
        rows = pl.ds(start, size)
        return functools.partial(pltpu.make_async_copy, act.at[rows], act_out.at[rows])

    def load_half(source, target, lane):
        return functools.partial(
            pltpu.make_async_copy,
            source.at[:, relative_half(part, wide)],
            target.at[:, pl.ds(lane, wide)],
        )

    matrices = [wk, wv]
    loads = [load_rows(*chunks[0])]
    loads += [load_half(w, held, at * wide) for at, w in enumerate(matrices)]
    loads += [load_rows(*chunk) for chunk in chunks[1:]]
    loads += [load_half(wq, wq_out, 0)]
    queue = [load(sems.at[at]) for at, load in enumerate(loads)]
    load_logs = pltpu.make_async_copy(decay, logs, sems.at[len(queue)])
    load_logs.start()
    for copy in queue[:AHEAD]:
        copy.start()

    def take(at):
        queue[at].wait()
        if at + AHEAD < len(queue):
            queue[at + AHEAD].start()

    load_logs.wait()
    rates = jnp.where(lax.axis_index("grp") == part, logs[:half], logs[half:])
    rates = jnp.concatenate([rates, jnp.zeros((8 - half, tokens), F32)], axis=0)
    stacked = jnp.concatenate([rates[:, n * BLOCK : (n + 1) * BLOCK] for n in range(blocks)], axis=0)
    upper = (
        lax.broadcasted_iota(jnp.int32, (BLOCK, BLOCK), 0)
        <= lax.broadcasted_iota(jnp.int32, (BLOCK, BLOCK), 1)
    ).astype(F32)
    within = LOG2E * dot(stacked, upper, precision=HIGHEST)
    total = jnp.zeros((8, 1), F32)
    for n in range(blocks):
        rows = within[n * 8 : (n + 1) * 8]
        wrow[n] = rows
        wcol[n] = rows.T
        reach[n] = jnp.broadcast_to(jnp.exp2(total), (8, DH))
        total = total + rows[:, BLOCK - 1 :]
    factor = jnp.broadcast_to(jnp.exp2(total), (8, DH))
    state[...] = jnp.zeros_like(state)

    for chunk, (start, size) in enumerate(chunks):
        rows = slice(start, start + size)
        take(chunk + len(matrices) if chunk else 0)
        halves = []
        for at in range(len(matrices)):
            if chunk == 0:
                take(1 + at)
            lanes = slice(at * wide, (at + 1) * wide)
            halves.append(dot(act_out[rows], held[:, lanes]).astype(BF16))
            kv_out[rows, lanes] = halves[at]
        for b in range(size // BLOCK):
            n = start // BLOCK + b
            block = slice(b * BLOCK, (b + 1) * BLOCK)
            for h in range(half):
                lanes = slice(h * DH, (h + 1) * DH)
                cols = jnp.broadcast_to(wcol[n][:, h : h + 1], (BLOCK, DH))
                spread[n, h] = cols
                last = cols[BLOCK - 1 :]
                k_b = halves[0][block, lanes].astype(F32) * jnp.exp2(last - cols)
                update = dot(k_b.astype(BF16), halves[1][block, lanes], ((0,), (0,)))
                old = state[h]
                before[n, h] = old
                state[h] = jnp.exp2(last) * old + update

    for h in range(half):
        payload[h, :DH] = state[h].astype(BF16)
        whole = jnp.broadcast_to(factor[h : h + 1], (EXTRA, DH))
        high = whole.astype(BF16).astype(F32)
        first = lax.broadcasted_iota(jnp.int32, (EXTRA, DH), 0) < EXTRA // 2
        payload[h, DH:] = jnp.where(first, high, whole - high).astype(BF16)
    take(len(queue) - 1)


def project_kernel(act, w, out):
    for step in range(act.shape[0] // STEP):
        rows = slice(step * STEP, (step + 1) * STEP)
        out[rows] = dot(act[rows], w[...]).astype(BF16)


def incoming_state(arrivals, h):
    place = lax.axis_index("seq")
    sources = [lax.bitwise_xor(place, r + 1) for r in range(len(arrivals))]
    reaches = []
    for piece in arrivals:
        extra = piece[h, DH:].astype(F32)
        reaches.append(extra[:1] + extra[EXTRA // 2 : EXTRA // 2 + 1])
    total = jnp.zeros((DH, DH), F32)
    for source, piece in zip(sources, arrivals):
        weight = jnp.where(source < place, jnp.ones((1, DH), F32), 0.0)
        for other, reach in zip(sources, reaches):
            between = jnp.logical_and(other > source, other < place)
            weight = weight * jnp.where(between, reach, 1.0)
        total = total + weight * piece[h, :DH].astype(F32)
    return total


def attend_kernel(received, q, kv, before, spread, wrow, reach, *rest):
    arrivals, (out, held, bound, sems) = rest[:received], rest[received:]
    sources, share, columns = out.shape
    heads = columns // DH

    def send(target):
        return pltpu.make_async_copy(held.at[target], out.at[target], sems.at[target])

    causal = lax.broadcasted_iota(jnp.int32, (BLOCK, BLOCK), 0) >= lax.broadcasted_iota(
        jnp.int32, (BLOCK, BLOCK), 1
    )
    bound[...] = jnp.where(causal, 0.0, -1e30)
    prefix = [incoming_state(arrivals, h) for h in range(heads)]

    @pl.loop(0, sources)
    def _(target):
        for b in range(share // BLOCK):
            n = target * (share // BLOCK) + b
            rows = pl.ds(pl.multiple_of(n * BLOCK, BLOCK), BLOCK)
            reached = reach[n]
            lanes = [slice(h * DH, (h + 1) * DH) for h in range(heads)]
            scores = [dot(q[rows, lane], kv[rows, lane], ((1,), (1,))) for lane in lanes]
            carried = []
            for h, lane in enumerate(lanes):
                incoming = (before[n, h] + reached[h : h + 1] * prefix[h]).astype(BF16)
                carried.append(dot(q[rows, lane], incoming))
            weights = []
            for h in range(heads):
                cols = spread[n, h]
                gap = jnp.concatenate([cols] * (BLOCK // DH), axis=1) - wrow[n, h : h + 1]
                weights.append((scores[h] * jnp.exp2(jnp.minimum(gap, bound[...]))).astype(BF16))
            for h, lane in enumerate(lanes):
                v_b = kv[rows, columns + h * DH : columns + (h + 1) * DH]
                attended = dot(weights[h], v_b) + jnp.exp2(spread[n, h]) * carried[h]
                mean = jnp.mean(attended * attended, axis=1, keepdims=True)
                normed = (attended * lax.rsqrt(mean + 1e-5)).astype(BF16)
                held[target, b * BLOCK : (b + 1) * BLOCK, lane] = normed
        send(target).start()

    for target in range(sources):
        send(target).wait()


def out_kernel(offsets, order, begun, features, *rest):
    if begun:
        earlier, rest = rest[0], rest[1:]
    weights, (out, left, held, ready, done, sems, out_sems) = rest[:-7], rest[-7:]
    mine, place = lax.axis_index("head"), lax.axis_index("seq")
    half = features.shape[2]
    width = done.shape[2]
    each = len(weights) // len(offsets)

    def store(slot):
        if not begun:
            return pltpu.make_async_copy(done.at[slot], out.at[slot], out_sems.at[slot])
        columns = pl.ds(pl.multiple_of(lax.bitwise_xor(place, offsets[slot]) * width, width), width)
        return pltpu.make_async_copy(done.at[slot], out.at[:, columns], out_sems.at[slot])

    loads, parts = [], []
    for slot in range(len(offsets)):
        begin = 0
        for piece in weights[slot * each : (slot + 1) * each]:
            rows = pl.ds(begin, piece.shape[0])
            parts.append((slot, rows, len(loads)))
            loads.append((piece, held.at[slot, rows]))
            begin += piece.shape[0]
        if begun:
            loads.append((earlier.at[slot], ready.at[slot]))
    queue = [pltpu.make_async_copy(*pair, sems.at[i]) for i, pair in enumerate(loads)]
    for copy in queue[:OUT_AHEAD]:
        copy.start()

    def take(i):
        queue[i].wait()
        if i + OUT_AHEAD < len(queue):
            queue[i + OUT_AHEAD].start()

    for i, r in enumerate(order):
        left[:, i * half : (i + 1) * half] = features[lax.bitwise_xor(mine, r)]
    for slot in range(len(offsets)):
        total = None
        for at, rows, i in parts:
            if at == slot:
                take(i)
                term = dot(left[:, rows], held[slot, rows])
                total = term if total is None else total + term
        if begun:
            take((slot + 1) * (each + 1) - 1)
            total = total + ready[slot]
        done[slot] = total.astype(done.dtype)
        store(slot).start()
    for slot in range(len(offsets)):
        store(slot).wait()


def cost(flops, moved):
    return pl.CostEstimate(flops=flops, bytes_accessed=moved, transcendentals=0)


def in_hbm():
    return pl.BlockSpec(memory_space=pltpu.HBM)


def stay_in_hbm(*values):
    return [pltpu.with_memory_space_constraint(value, pltpu.HBM) for value in values]


def in_vmem():
    return pl.BlockSpec(memory_space=pltpu.VMEM)


def keys_values(part, activations, w_key, w_value, w_query, log_decay):
    tokens, width = activations.shape
    heads = log_decay.shape[0] // 2
    columns, blocks = heads * DH, tokens // BLOCK
    shapes = [
        ((tokens, width), BF16),
        ((width, columns), BF16),
        ((tokens, 2 * columns), BF16),
        ((blocks, heads, DH, DH), F32),
        ((heads, DH + EXTRA, DH), BF16),
        ((blocks, heads, BLOCK, DH), F32),
        ((blocks, 8, BLOCK), F32),
        ((blocks, 8, DH), F32),
    ]
    return pl.pallas_call(
        functools.partial(kv_kernel, part),
        in_specs=[in_hbm()] * 5,
        out_specs=[in_vmem()] * len(shapes),
        out_shape=[pltpu.VMEM(*shape) for shape in shapes],
        scratch_shapes=[
            pltpu.VMEM((width, 2 * columns), BF16),
            pltpu.VMEM((2 * heads, tokens), F32),
            pltpu.VMEM((heads, DH, DH), F32),
            pltpu.VMEM((blocks, BLOCK, 8), F32),
            pltpu.SemaphoreType.DMA((tokens // BLOCK + 4,)),
        ],
        compiler_params=pltpu.CompilerParams(vmem_limit_bytes=16 * MIB),
        cost_estimate=cost(4 * tokens * width * columns, 4 * tokens * width),
        name="keys_values",
    )(*stay_in_hbm(activations, w_key, w_value, w_query, log_decay))


def queries(activations, w_query):
    tokens, width = activations.shape
    columns = w_query.shape[1]
    return pl.pallas_call(
        project_kernel,
        in_specs=[in_vmem()] * 2,
        out_specs=in_vmem(),
        out_shape=pltpu.VMEM((tokens, columns), BF16),
        compiler_params=pltpu.CompilerParams(vmem_limit_bytes=16 * MIB),
        cost_estimate=cost(2 * tokens * width * columns, 2 * tokens * width),
        name="queries",
    )(activations, w_query)


def attend(sources, query, *rest):
    received = len(rest) - 5
    tokens, columns = query.shape
    shares = (sources, tokens // sources, columns)
    return pl.pallas_call(
        functools.partial(attend_kernel, received),
        in_specs=[in_vmem()] * (len(rest) + 1),
        out_specs=in_hbm(),
        out_shape=pltpu.HBM(shares, BF16),
        scratch_shapes=[
            pltpu.VMEM(shares, BF16),
            pltpu.VMEM((BLOCK, BLOCK), F32),
            pltpu.SemaphoreType.DMA((sources,)),
        ],
        compiler_params=pltpu.CompilerParams(vmem_limit_bytes=16 * MIB),
        cost_estimate=cost(20 * tokens * BLOCK * columns, 8 * tokens * columns),
        name="attend",
    )(query, *rest)


def swap(value, axis, bit):
    count = lax.axis_size(axis)
    return lax.ppermute(value, axis, [(i, i ^ bit) for i in range(count)])


def bits_of(count):
    return [1 << b for b in reversed(range(count.bit_length() - 1))]


def gather_rows(w_out):
    half = w_out.shape[0] // 2
    own = lax.dynamic_slice_in_dim(w_out, lax.axis_index("grp") * half, half, axis=0)
    return {0: own} | {bit: swap(own, "head", bit) for bit in bits_of(lax.axis_size("head"))}


def gather_rest(pieces):
    pieces = dict(pieces)
    for r in range(lax.axis_size("head")):
        if r not in pieces:
            pieces[r] = swap(pieces[r & (r - 1)], "head", r & -r)
    return pieces


def gather_columns(even, odd, even_across, even_beside, settled):
    across, beside = [even_across], [even_beside]
    even_beside, odd = after((even_beside, odd), *settled)
    odd_across, odd_beside = lax.optimization_barrier((swap(odd, "seq", 2), swap(odd, "grp", 1)))
    across.append(odd_across)
    beside.append(odd_beside)
    corner = [swap(even_beside, "seq", 2), swap(across[1], "grp", 1)]
    found = {(0, 0): [even, odd], (0, 2): across, (1, 0): beside, (1, 2): corner}
    for bit in bits_of(lax.axis_size("seq"))[:-2]:
        found.update(
            {
                (g, s ^ bit): [swap(part, "seq", bit) for part in parts]
                for (g, s), parts in list(found.items())
            }
        )
    return found


def gather_partner(found):
    return found | {
        (g, s ^ 1): [swap(part, "seq", 1) for part in parts] for (g, s), parts in found.items()
    }


def project_out(features, part, found, order, earlier=None):
    sources, rows, columns = features.shape
    offsets = sorted({s for _, s in found})
    operands = [piece for offset in offsets for piece in found[(part, offset)]]
    width, blocks = operands[0].shape[1], len(offsets)
    lead = [] if earlier is None else [earlier]
    shape = (rows, blocks * width) if lead else (blocks, rows, width)
    dtype = BF16 if lead else F32
    return pl.pallas_call(
        functools.partial(out_kernel, offsets, order, bool(lead)),
        out_shape=pltpu.HBM(shape, dtype),
        in_specs=[in_vmem()] + [in_hbm()] * (len(lead) + len(operands)),
        out_specs=in_hbm(),
        scratch_shapes=[
            pltpu.VMEM((rows, sources * columns), BF16),
            pltpu.VMEM((blocks, sources * columns, width), BF16),
            pltpu.VMEM((blocks, rows, width) if lead else (8, 128), F32),
            pltpu.VMEM((blocks, rows, width), dtype),
            pltpu.SemaphoreType.DMA((len(operands) + blocks * len(lead),)),
            pltpu.SemaphoreType.DMA((blocks,)),
        ],
        compiler_params=pltpu.CompilerParams(vmem_limit_bytes=24 * MIB),
        cost_estimate=cost(2 * rows * sources * columns * width * blocks, 8 * MIB),
        name="project_out",
    )(features, *stay_in_hbm(*lead, *operands))


def after(value, *earlier):
    return lax.optimization_barrier((value, *earlier))[0]


def on_device(activations, w_query, w_key, w_value, w_out, log_decay):
    places, sources = lax.axis_size("seq"), lax.axis_size("head")
    pieces = gather_rows(w_out)
    features = []
    for part in range(2):
        rows, w_part, kv, before, payload, spread, wrow, reach = keys_values(
            part, activations, w_key, w_value, w_query, log_decay
        )
        arrivals = [swap(payload, "seq", r) for r in range(1, places)]
        if part == 0:
            rows, pieces = lax.optimization_barrier((rows, pieces))
            pieces = gather_rest(pieces)
        else:
            rows, across, beside = lax.optimization_barrier((rows, across, beside))
        query = queries(rows, w_part)
        normed = attend(sources, query, kv, before, spread, wrow, reach, *arrivals)
        if part == 0:
            normed, pieces, activations = lax.optimization_barrier((normed, pieces, activations))
            even, odd = [r for r in pieces if r % 2 == 0], [r for r in pieces if r % 2]
            order = even + odd
            even, odd = [
                jnp.concatenate([pieces[r] for r in group], axis=0) for group in (even, odd)
            ]
            across, beside = swap(even, "seq", 2), swap(even, "grp", 1)
        features.append(lax.all_to_all(normed, "head", 0, 0))
    found = gather_columns(even, odd, across, beside, [query, *arrivals])
    first = {(g, s): parts for (g, s), parts in found.items() if g == 0}
    begun = project_out(features[0], 0, gather_partner(first), order)
    second = {(g, s): parts for (g, s), parts in found.items() if g == 1}
    second, begun = lax.optimization_barrier((second, begun))
    return project_out(features[1], 1, gather_partner(second), order, begun)


def solution(mesh):
    return jax.shard_map(
        on_device,
        mesh=mesh,
        in_specs=(
            P(("grp", "seq"), None),
            P(None, "head"),
            P(None, "head"),
            P(None, "head"),
            P("head", "seq"),
            P("head", ("grp", "seq")),
        ),
        out_specs=P(("grp", "seq", "head"), None),
        check_vma=False,
    )
```

```python
import functools

import jax
import jax.numpy as jnp
from jax import lax
from jax.experimental import pallas as pl
from jax.experimental.pallas import tpu as pltpu
from jax.sharding import PartitionSpec as P

DH = 128
BLOCK = 256
STEP = 512
AHEAD = 3
OUT_AHEAD = 8
EXTRA = 16
F32 = jnp.float32
BF16 = jnp.bfloat16
HIGHEST = lax.Precision.HIGHEST
LOG2E = 1.4426950408889634
MIB = 1 << 20


def dot(a, b, dims=((1,), (0,)), precision=None):
    return lax.dot_general(a, b, (dims, ((), ())), precision=precision, preferred_element_type=F32)


def relative_half(part, width):
    start = lax.rem(part + lax.axis_index("grp"), 2) * width
    return pl.ds(pl.multiple_of(start, width), width)


def kv_kernel(part, act, wk, wv, wq, decay, act_out, wq_out, kv_out, before, payload, spread, wrow, reach,
              held, logs, state, wcol, sems):
    half, tokens = decay.shape[0] // 2, decay.shape[1]
    blocks = tokens // BLOCK
    wide = half * DH
    chunks = [(0, BLOCK)]
    while sum(chunks[-1]) < tokens:
        start = sum(chunks[-1])
        chunks.append((start, min(start, tokens - start)))

    def load_rows(start, size):
        rows = pl.ds(start, size)
        return functools.partial(pltpu.make_async_copy, act.at[rows], act_out.at[rows])

    def load_half(source, target, lane):
        return functools.partial(
            pltpu.make_async_copy,
            source.at[:, relative_half(part, wide)],
            target.at[:, pl.ds(lane, wide)],
        )

    matrices = [wk, wv]
    loads = [load_rows(*chunks[0])]
    loads += [load_half(w, held, at * wide) for at, w in enumerate(matrices)]
    loads += [load_rows(*chunk) for chunk in chunks[1:]]
    loads += [load_half(wq, wq_out, 0)]
    queue = [load(sems.at[at]) for at, load in enumerate(loads)]
    load_logs = pltpu.make_async_copy(decay, logs, sems.at[len(queue)])
    load_logs.start()
    for copy in queue[:AHEAD]:
        copy.start()

    def take(at):
        queue[at].wait()
        if at + AHEAD < len(queue):
            queue[at + AHEAD].start()

    load_logs.wait()
    rates = jnp.where(lax.axis_index("grp") == part, logs[:half], logs[half:])
    rates = jnp.concatenate([rates, jnp.zeros((8 - half, tokens), F32)], axis=0)
    stacked = jnp.concatenate([rates[:, n * BLOCK : (n + 1) * BLOCK] for n in range(blocks)], axis=0)
    upper = (
        lax.broadcasted_iota(jnp.int32, (BLOCK, BLOCK), 0)
        <= lax.broadcasted_iota(jnp.int32, (BLOCK, BLOCK), 1)
    ).astype(F32)
    within = LOG2E * dot(stacked, upper, precision=HIGHEST)
    total = jnp.zeros((8, 1), F32)
    for n in range(blocks):
        rows = within[n * 8 : (n + 1) * 8]
        wrow[n] = rows
        wcol[n] = rows.T
        reach[n] = jnp.broadcast_to(jnp.exp2(total), (8, DH))
        total = total + rows[:, BLOCK - 1 :]
    factor = jnp.broadcast_to(jnp.exp2(total), (8, DH))
    state[...] = jnp.zeros_like(state)

    for chunk, (start, size) in enumerate(chunks):
        rows = slice(start, start + size)
        take(chunk + len(matrices) if chunk else 0)
        halves = []
        for at in range(len(matrices)):
            if chunk == 0:
                take(1 + at)
            lanes = slice(at * wide, (at + 1) * wide)
            halves.append(dot(act_out[rows], held[:, lanes]).astype(BF16))
            kv_out[rows, lanes] = halves[at]
        for b in range(size // BLOCK):
            n = start // BLOCK + b
            block = slice(b * BLOCK, (b + 1) * BLOCK)
            for h in range(half):
                lanes = slice(h * DH, (h + 1) * DH)
                cols = jnp.broadcast_to(wcol[n][:, h : h + 1], (BLOCK, DH))
                spread[n, h] = cols
                last = cols[BLOCK - 1 :]
                k_b = halves[0][block, lanes].astype(F32) * jnp.exp2(last - cols)
                update = dot(k_b.astype(BF16), halves[1][block, lanes], ((0,), (0,)))
                old = state[h]
                before[n, h] = old
                state[h] = jnp.exp2(last) * old + update

    for h in range(half):
        payload[h, :DH] = state[h].astype(BF16)
        whole = jnp.broadcast_to(factor[h : h + 1], (EXTRA, DH))
        high = whole.astype(BF16).astype(F32)
        first = lax.broadcasted_iota(jnp.int32, (EXTRA, DH), 0) < EXTRA // 2
        payload[h, DH:] = jnp.where(first, high, whole - high).astype(BF16)
    take(len(queue) - 1)


def project_kernel(act, w, out):
    for step in range(act.shape[0] // STEP):
        rows = slice(step * STEP, (step + 1) * STEP)
        out[rows] = dot(act[rows], w[...]).astype(BF16)


def incoming_state(arrivals, h):
    place = lax.axis_index("seq")
    sources = [lax.bitwise_xor(place, r + 1) for r in range(len(arrivals))]
    reaches = []
    for piece in arrivals:
        extra = piece[h, DH:].astype(F32)
        reaches.append(extra[:1] + extra[EXTRA // 2 : EXTRA // 2 + 1])
    total = jnp.zeros((DH, DH), F32)
    for source, piece in zip(sources, arrivals):
        weight = jnp.where(source < place, jnp.ones((1, DH), F32), 0.0)
        for other, reach in zip(sources, reaches):
            between = jnp.logical_and(other > source, other < place)
            weight = weight * jnp.where(between, reach, 1.0)
        total = total + weight * piece[h, :DH].astype(F32)
    return total


def attend_kernel(received, q, kv, before, spread, wrow, reach, *rest):
    arrivals, (out, held, bound, sems) = rest[:received], rest[received:]
    sources, share, columns = out.shape
    heads = columns // DH

    def send(target):
        return pltpu.make_async_copy(held.at[target], out.at[target], sems.at[target])

    causal = lax.broadcasted_iota(jnp.int32, (BLOCK, BLOCK), 0) >= lax.broadcasted_iota(
        jnp.int32, (BLOCK, BLOCK), 1
    )
    bound[...] = jnp.where(causal, 0.0, -1e30)
    prefix = [incoming_state(arrivals, h) for h in range(heads)]

    @pl.loop(0, sources)
    def _(target):
        chains = []
        for b in range(share // BLOCK):
            n = target * (share // BLOCK) + b
            rows = pl.ds(pl.multiple_of(n * BLOCK, BLOCK), BLOCK)
            chains += [(b, n, rows, h, slice(h * DH, (h + 1) * DH)) for h in range(heads)]
        scores = [dot(q[rows, lane], kv[rows, lane], ((1,), (1,))) for _, _, rows, _, lane in chains]
        carried = []
        for _, n, rows, h, lane in chains:
            incoming = (before[n, h] + reach[n, h : h + 1] * prefix[h]).astype(BF16)
            carried.append(dot(q[rows, lane], incoming))
        weights = []
        for score, (_, n, _, h, _) in zip(scores, chains):
            gap = jnp.concatenate([spread[n, h]] * (BLOCK // DH), axis=1) - wrow[n, h : h + 1]
            weights.append((score * jnp.exp2(jnp.minimum(gap, bound[...]))).astype(BF16))
        for weight, late, (b, n, rows, h, lane) in zip(weights, carried, chains):
            v_b = kv[rows, columns + h * DH : columns + (h + 1) * DH]
            attended = dot(weight, v_b) + jnp.exp2(spread[n, h]) * late
            mean = jnp.mean(attended * attended, axis=1, keepdims=True)
            normed = (attended * lax.rsqrt(mean + 1e-5)).astype(BF16)
            held[target, b * BLOCK : (b + 1) * BLOCK, lane] = normed
        send(target).start()

    for target in range(sources):
        send(target).wait()


def out_kernel(offsets, order, begun, features, *rest):
    if begun:
        earlier, rest = rest[0], rest[1:]
    weights, (out, left, held, ready, done, sems, out_sems) = rest[:-7], rest[-7:]
    mine, place = lax.axis_index("head"), lax.axis_index("seq")
    half = features.shape[2]
    width = done.shape[2]
    each = len(weights) // len(offsets)

    def store(slot):
        if not begun:
            return pltpu.make_async_copy(done.at[slot], out.at[slot], out_sems.at[slot])
        columns = pl.ds(pl.multiple_of(lax.bitwise_xor(place, offsets[slot]) * width, width), width)
        return pltpu.make_async_copy(done.at[slot], out.at[:, columns], out_sems.at[slot])

    loads, parts = [], []
    for slot in range(len(offsets)):
        begin = 0
        for piece in weights[slot * each : (slot + 1) * each]:
            rows = pl.ds(begin, piece.shape[0])
            parts.append((slot, rows, len(loads)))
            loads.append((piece, held.at[slot, rows]))
            begin += piece.shape[0]
        if begun:
            loads.append((earlier.at[slot], ready.at[slot]))
    queue = [pltpu.make_async_copy(*pair, sems.at[i]) for i, pair in enumerate(loads)]
    for copy in queue[:OUT_AHEAD]:
        copy.start()

    def take(i):
        queue[i].wait()
        if i + OUT_AHEAD < len(queue):
            queue[i + OUT_AHEAD].start()

    for i, r in enumerate(order):
        left[:, i * half : (i + 1) * half] = features[lax.bitwise_xor(mine, r)]
    for slot in range(len(offsets)):
        total = None
        for at, rows, i in parts:
            if at == slot:
                take(i)
                term = dot(left[:, rows], held[slot, rows])
                total = term if total is None else total + term
        if begun:
            take((slot + 1) * (each + 1) - 1)
            total = total + ready[slot]
        done[slot] = total.astype(done.dtype)
        store(slot).start()
    for slot in range(len(offsets)):
        store(slot).wait()


def cost(flops, moved):
    return pl.CostEstimate(flops=flops, bytes_accessed=moved, transcendentals=0)


def in_hbm():
    return pl.BlockSpec(memory_space=pltpu.HBM)


def stay_in_hbm(*values):
    return [pltpu.with_memory_space_constraint(value, pltpu.HBM) for value in values]


def in_vmem():
    return pl.BlockSpec(memory_space=pltpu.VMEM)


def keys_values(part, activations, w_key, w_value, w_query, log_decay):
    tokens, width = activations.shape
    heads = log_decay.shape[0] // 2
    columns, blocks = heads * DH, tokens // BLOCK
    shapes = [
        ((tokens, width), BF16),
        ((width, columns), BF16),
        ((tokens, 2 * columns), BF16),
        ((blocks, heads, DH, DH), F32),
        ((heads, DH + EXTRA, DH), BF16),
        ((blocks, heads, BLOCK, DH), F32),
        ((blocks, 8, BLOCK), F32),
        ((blocks, 8, DH), F32),
    ]
    return pl.pallas_call(
        functools.partial(kv_kernel, part),
        in_specs=[in_hbm()] * 5,
        out_specs=[in_vmem()] * len(shapes),
        out_shape=[pltpu.VMEM(*shape) for shape in shapes],
        scratch_shapes=[
            pltpu.VMEM((width, 2 * columns), BF16),
            pltpu.VMEM((2 * heads, tokens), F32),
            pltpu.VMEM((heads, DH, DH), F32),
            pltpu.VMEM((blocks, BLOCK, 8), F32),
            pltpu.SemaphoreType.DMA((tokens // BLOCK + 4,)),
        ],
        compiler_params=pltpu.CompilerParams(vmem_limit_bytes=16 * MIB),
        cost_estimate=cost(4 * tokens * width * columns, 4 * tokens * width),
        name="keys_values",
    )(*stay_in_hbm(activations, w_key, w_value, w_query, log_decay))


def queries(activations, w_query):
    tokens, width = activations.shape
    columns = w_query.shape[1]
    return pl.pallas_call(
        project_kernel,
        in_specs=[in_vmem()] * 2,
        out_specs=in_vmem(),
        out_shape=pltpu.VMEM((tokens, columns), BF16),
        compiler_params=pltpu.CompilerParams(vmem_limit_bytes=16 * MIB),
        cost_estimate=cost(2 * tokens * width * columns, 2 * tokens * width),
        name="queries",
    )(activations, w_query)


def attend(sources, query, *rest):
    received = len(rest) - 5
    tokens, columns = query.shape
    shares = (sources, tokens // sources, columns)
    return pl.pallas_call(
        functools.partial(attend_kernel, received),
        in_specs=[in_vmem()] * (len(rest) + 1),
        out_specs=in_hbm(),
        out_shape=pltpu.HBM(shares, BF16),
        scratch_shapes=[
            pltpu.VMEM(shares, BF16),
            pltpu.VMEM((BLOCK, BLOCK), F32),
            pltpu.SemaphoreType.DMA((sources,)),
        ],
        compiler_params=pltpu.CompilerParams(vmem_limit_bytes=16 * MIB),
        cost_estimate=cost(20 * tokens * BLOCK * columns, 8 * tokens * columns),
        name="attend",
    )(query, *rest)


def swap(value, axis, bit):
    count = lax.axis_size(axis)
    return lax.ppermute(value, axis, [(i, i ^ bit) for i in range(count)])


def bits_of(count):
    return [1 << b for b in reversed(range(count.bit_length() - 1))]


def gather_rows(w_out):
    half = w_out.shape[0] // 2
    own = lax.dynamic_slice_in_dim(w_out, lax.axis_index("grp") * half, half, axis=0)
    return {0: own} | {bit: swap(own, "head", bit) for bit in bits_of(lax.axis_size("head"))}


def gather_rest(pieces):
    pieces = dict(pieces)
    for r in range(lax.axis_size("head")):
        if r not in pieces:
            pieces[r] = swap(pieces[r & (r - 1)], "head", r & -r)
    return pieces


def gather_columns(even, odd, even_across, even_beside, settled):
    across, beside = [even_across], [even_beside]
    even_beside, odd = after((even_beside, odd), *settled)
    odd_across, odd_beside = lax.optimization_barrier((swap(odd, "seq", 2), swap(odd, "grp", 1)))
    across.append(odd_across)
    beside.append(odd_beside)
    corner = [swap(even_beside, "seq", 2), swap(across[1], "grp", 1)]
    found = {(0, 0): [even, odd], (0, 2): across, (1, 0): beside, (1, 2): corner}
    for bit in bits_of(lax.axis_size("seq"))[:-2]:
        found.update(
            {
                (g, s ^ bit): [swap(part, "seq", bit) for part in parts]
                for (g, s), parts in list(found.items())
            }
        )
    return found


def gather_partner(found):
    return found | {
        (g, s ^ 1): [swap(part, "seq", 1) for part in parts] for (g, s), parts in found.items()
    }


def project_out(features, part, found, order, earlier=None):
    sources, rows, columns = features.shape
    offsets = sorted({s for _, s in found})
    operands = [piece for offset in offsets for piece in found[(part, offset)]]
    width, blocks = operands[0].shape[1], len(offsets)
    lead = [] if earlier is None else [earlier]
    shape = (rows, blocks * width) if lead else (blocks, rows, width)
    dtype = BF16 if lead else F32
    return pl.pallas_call(
        functools.partial(out_kernel, offsets, order, bool(lead)),
        out_shape=pltpu.HBM(shape, dtype),
        in_specs=[in_vmem()] + [in_hbm()] * (len(lead) + len(operands)),
        out_specs=in_hbm(),
        scratch_shapes=[
            pltpu.VMEM((rows, sources * columns), BF16),
            pltpu.VMEM((blocks, sources * columns, width), BF16),
            pltpu.VMEM((blocks, rows, width) if lead else (8, 128), F32),
            pltpu.VMEM((blocks, rows, width), dtype),
            pltpu.SemaphoreType.DMA((len(operands) + blocks * len(lead),)),
            pltpu.SemaphoreType.DMA((blocks,)),
        ],
        compiler_params=pltpu.CompilerParams(vmem_limit_bytes=24 * MIB),
        cost_estimate=cost(2 * rows * sources * columns * width * blocks, 8 * MIB),
        name="project_out",
    )(features, *stay_in_hbm(*lead, *operands))


def after(value, *earlier):
    return lax.optimization_barrier((value, *earlier))[0]


def on_device(activations, w_query, w_key, w_value, w_out, log_decay):
    places, sources = lax.axis_size("seq"), lax.axis_size("head")
    pieces = gather_rows(w_out)
    features = []
    for part in range(2):
        rows, w_part, kv, before, payload, spread, wrow, reach = keys_values(
            part, activations, w_key, w_value, w_query, log_decay
        )
        arrivals = [swap(payload, "seq", r) for r in range(1, places)]
        if part == 0:
            rows, pieces = lax.optimization_barrier((rows, pieces))
            pieces = gather_rest(pieces)
        else:
            rows, across, beside = lax.optimization_barrier((rows, across, beside))
        query = queries(rows, w_part)
        normed = attend(sources, query, kv, before, spread, wrow, reach, *arrivals)
        if part == 0:
            normed, pieces, activations = lax.optimization_barrier((normed, pieces, activations))
            even, odd = [r for r in pieces if r % 2 == 0], [r for r in pieces if r % 2]
            order = even + odd
            even, odd = [
                jnp.concatenate([pieces[r] for r in group], axis=0) for group in (even, odd)
            ]
            across, beside = swap(even, "seq", 2), swap(even, "grp", 1)
        features.append(lax.all_to_all(normed, "head", 0, 0))
    found = gather_columns(even, odd, across, beside, [query, *arrivals])
    first = {(g, s): parts for (g, s), parts in found.items() if g == 0}
    begun = project_out(features[0], 0, gather_partner(first), order)
    second = {(g, s): parts for (g, s), parts in found.items() if g == 1}
    second, begun = lax.optimization_barrier((second, begun))
    return project_out(features[1], 1, gather_partner(second), order, begun)


def solution(mesh):
    return jax.shard_map(
        on_device,
        mesh=mesh,
        in_specs=(
            P(("grp", "seq"), None),
            P(None, "head"),
            P(None, "head"),
            P(None, "head"),
            P("head", "seq"),
            P("head", ("grp", "seq")),
        ),
        out_specs=P(("grp", "seq", "head"), None),
        check_vma=False,
    )
```
